32 devices in a mesh: seq: 8 (over y, x, core), fsdp: 4 (over z).
Axes of the slice: x: 2, y: 2, z: 4, core: 2. Of those that a mesh axis runs over, the one named last changes fastest.
Arguments:
- tokens: bfloat16 [4, 8192, 640], P('fsdp', 'seq'), may hold values from -16 to 16
- document_ids: int32 [4, 8192], P('fsdp'), may hold values from 0 to 1, as said below
- cotangent: bfloat16 [4, 8192, 640], P('fsdp', 'seq'), may hold values from -6 to 6
- w_query: bfloat16 [640, 1024], P('fsdp'), may hold values from -0.25 to 0.25
- w_key: bfloat16 [640, 256], P('fsdp'), may hold values from -0.25 to 0.25
- w_value: bfloat16 [640, 256], P('fsdp'), may hold values from -0.25 to 0.25
- w_out: bfloat16 [1024, 640], P('fsdp'), may hold values from -0.375 to 0.375
- w_gate: bfloat16 [640, 2048], P('fsdp'), may hold values from -0.25 to 0.25
- w_up: bfloat16 [640, 2048], P('fsdp'), may hold values from -0.25 to 0.25
- w_down: bfloat16 [2048, 640], P('fsdp'), may hold values from -0.125 to 0.125
- gain_attn_in: bfloat16 [640], P('fsdp'), may hold values from 0.5 to 1.5
- gain_attn_out: bfloat16 [640], P('fsdp'), may hold values from 0.5 to 1.5
- gain_ffn_in: bfloat16 [640], P('fsdp'), may hold values from 0.5 to 1.5
- gain_ffn_out: bfloat16 [640], P('fsdp'), may hold values from 0.5 to 1.5
- gain_query: bfloat16 [256], P('fsdp'), may hold values from 0.5 to 1.5
- gain_key: bfloat16 [256], P('fsdp'), may hold values from 0.5 to 1.5
Outputs:
- output: bfloat16 [4, 8192, 640], P('fsdp', 'seq')
- input_grad: float32 [4, 8192, 640], P('fsdp', 'seq')
- grad_w_query: float32 [640, 1024], P('fsdp')
- grad_w_key: float32 [640, 256], P('fsdp')
- grad_w_value: float32 [640, 256], P('fsdp')
- grad_w_out: float32 [1024, 640], P('fsdp')
- grad_w_gate: float32 [640, 2048], P('fsdp')
- grad_w_up: float32 [640, 2048], P('fsdp')
- grad_w_down: float32 [2048, 640], P('fsdp')
- grad_gain_attn_in: float32 [640], P('fsdp')
- grad_gain_attn_out: float32 [640], P('fsdp')
- grad_gain_ffn_in: float32 [640], P('fsdp')
- grad_gain_ffn_out: float32 [640], P('fsdp')
- grad_gain_query: float32 [256], P('fsdp')
- grad_gain_key: float32 [256], P('fsdp')
The draws below stay inside these ranges and needn't reach their ends.
Inputs may be any that keep to these rules, and one draw needn't show every extreme that they name: `document_ids`: in each group the ids never fall along the tokens, and the group holds exactly two documents, each of at least 2048 tokens.
All inputs are finite; a program needn't handle non-finite values.
Results may differ from the reference program's by a relative error of at most 0.017.
Values may be sent and summed in bfloat16 or wider, within the bound.
No kernel may reach another device: no remote copies, remote signals or barrier semaphores. Data moves between devices by JAX's collectives and lax.ppermute only.
A program may use at most 192 MiB of HBM per device.

```python
import math
import jax
import jax.numpy as jnp
from jax import lax

D = 640
HEADS = 4
HD = 256
FF = 2048
WINDOW = 512
QBLK = 512
GROUP_TOK = 8192
GROUPS = 4


def draw_tokens(key, part):
    noise_key, column_key, row_key = jax.random.split(key, 3)
    full_shape = (GROUPS, GROUP_TOK, D)
    column_scale = jnp.exp(jax.random.uniform(column_key, (D,), jnp.float32, math.log(0.3), math.log(3.0)))
    row_scale = jnp.exp(jax.random.uniform(row_key, (GROUPS, GROUP_TOK, 1), jnp.float32, math.log(0.5), math.log(2.0)))
    base_values = jax.random.normal(noise_key, full_shape, jnp.float32)
    return jnp.clip(base_values * column_scale * row_scale, -16.0, 16.0).astype(jnp.bfloat16)


def draw_document_ids(key, part):
    boundary = jax.random.randint(key, (GROUPS, 1), GROUP_TOK // 4, 3 * GROUP_TOK // 4 + 1, jnp.int32)
    places = jnp.arange(GROUP_TOK, dtype=jnp.int32)[None, :]
    return (places >= boundary).astype(jnp.int32)


def shard_levels(rng, shape, shards, low, high):
    level, own = 1.0, jax.random.fold_in(rng, 6)
    for axis_at, blocks in shards:
        draws = jnp.exp(jax.random.uniform(jax.random.fold_in(own, axis_at), (blocks,), jnp.float32, low / len(shards), high / len(shards)))
        level = level * jnp.repeat(draws, shape[axis_at] // blocks).reshape([-1 if axis == axis_at else 1 for axis in range(len(shape))])
    return level


def normal_values(stream_key, dims, scale, most, pieces=(), held_as=jnp.bfloat16):
    entries = jax.random.normal(stream_key, dims, jnp.float32) * scale
    if len(pieces) > 0:
        entries = shard_levels(stream_key, dims, pieces, -0.22, 0.18) * entries
    return jnp.clip(entries, min=-most, max=most).astype(held_as)


def setup_inputs(seed: int = 0) -> dict:
    keys = jax.random.split(jax.random.key(seed), 17)
    tokens = draw_tokens(jax.random.fold_in(keys[16], 71), 0)
    document_ids = draw_document_ids(jax.random.fold_in(keys[16], 71), 0)
    cotangent = normal_values(keys[2], (GROUPS, GROUP_TOK, D), 1.0, 6.0, ((0, 4), (1, 8)))
    w_query = normal_values(keys[3], (D, HEADS * HD), D ** -0.5, 0.25, ((0, 4),))
    w_key = normal_values(keys[4], (D, HD), D ** -0.5, 0.25, ((0, 4),))
    w_value = normal_values(keys[5], (D, HD), D ** -0.5, 0.25, ((0, 4),))
    w_out = normal_values(keys[6], (HEADS * HD, D), HD ** -0.5, 0.375, ((0, 4),))
    w_gate = normal_values(keys[7], (D, FF), D ** -0.5, 0.25, ((0, 4),))
    w_up = normal_values(keys[8], (D, FF), D ** -0.5, 0.25, ((0, 4),))
    w_down = normal_values(keys[9], (FF, D), FF ** -0.5, 0.125, ((0, 4),))
    gain_attn_in = jnp.clip(1.0 + 0.1 * jax.random.normal(keys[10], (D,), jnp.float32), 0.5, 1.5).astype(jnp.bfloat16)
    gain_attn_out = jnp.clip(1.0 + 0.1 * jax.random.normal(keys[11], (D,), jnp.float32), 0.5, 1.5).astype(jnp.bfloat16)
    gain_ffn_in = jnp.clip(1.0 + 0.1 * jax.random.normal(keys[12], (D,), jnp.float32), 0.5, 1.5).astype(jnp.bfloat16)
    gain_ffn_out = jnp.clip(1.0 + 0.1 * jax.random.normal(keys[13], (D,), jnp.float32), 0.5, 1.5).astype(jnp.bfloat16)
    gain_query = jnp.clip(1.0 + 0.1 * jax.random.normal(keys[14], (HD,), jnp.float32), 0.5, 1.5).astype(jnp.bfloat16)
    gain_key = jnp.clip(1.0 + 0.1 * jax.random.normal(keys[15], (HD,), jnp.float32), 0.5, 1.5).astype(jnp.bfloat16)
    return {"tokens": tokens, "document_ids": document_ids, "cotangent": cotangent, "w_query": w_query, "w_key": w_key, "w_value": w_value, "w_out": w_out, "w_gate": w_gate, "w_up": w_up, "w_down": w_down, "gain_attn_in": gain_attn_in, "gain_attn_out": gain_attn_out, "gain_ffn_in": gain_ffn_in, "gain_ffn_out": gain_ffn_out, "gain_query": gain_query, "gain_key": gain_key}


norm_epsilon = 1e-06
rope_base = 10000.0
score_scale = 0.0625
mask_fill = -1e+30
highest = lax.Precision.HIGHEST

@jax.custom_vjp
def low(v):
    return lax.optimization_barrier(v.astype(jnp.bfloat16)).astype(jnp.float32)

@jax.custom_vjp
def low_back(v):
    return v

def low_keep(v):
    return (low(v), None)

def low_pass(kept, grad):
    return (grad,)

def back_keep(v):
    return (v, None)

def back_low(kept, grad):
    return (low(grad),)
low.defvjp(low_keep, low_pass)
low_back.defvjp(back_keep, back_low)

def rms_scale(values, gain_vec):
    return values * lax.rsqrt(lax.optimization_barrier(jnp.mean(values * values, axis=-1, keepdims=True)) + norm_epsilon) * gain_vec

def rope_angles(positions):
    freq_steps = jnp.arange(0, HD, 2).astype(jnp.float32) / HD
    inverse = jnp.exp(-jnp.log(rope_base) * freq_steps)
    angles = positions.astype(jnp.float32)[:, None] * inverse[None, :]
    return (jnp.cos(angles), jnp.sin(angles))

def rotate(values, cosine, sine_part):
    half_width = values.shape[-1] // 2
    first_half = values[..., :half_width]
    second_half = values[..., half_width:]
    return jnp.concatenate([first_half * cosine - second_half * sine_part, second_half * cosine + first_half * sine_part], axis=-1)

def attend(queries, key_rows, value_rows, doc_rows):
    length = queries.shape[0]
    key_pad = jnp.concatenate([jnp.zeros((WINDOW, HD), jnp.float32), key_rows], axis=0)
    value_pad = jnp.concatenate([jnp.zeros((WINDOW, HD), jnp.float32), value_rows], axis=0)
    pad_ids = jnp.concatenate([jnp.full((WINDOW,), -1, jnp.int32), doc_rows], axis=0)
    offsets = jnp.arange(QBLK + WINDOW, dtype=jnp.int32)[None, :] - jnp.arange(QBLK, dtype=jnp.int32)[:, None]
    inside = (offsets >= 1) & (offsets <= WINDOW)

    @jax.checkpoint
    def one_block(block_start):
        query_block = lax.dynamic_slice_in_dim(queries, block_start, QBLK, 0)
        key_block = lax.dynamic_slice_in_dim(key_pad, block_start, QBLK + WINDOW, 0)
        value_block = lax.dynamic_slice_in_dim(value_pad, block_start, QBLK + WINDOW, 0)
        key_ids = lax.dynamic_slice_in_dim(pad_ids, block_start, QBLK + WINDOW, 0)
        query_ids = lax.dynamic_slice_in_dim(doc_rows, block_start, QBLK, 0)
        scores = low_back(jnp.einsum('qhd,kd->hqk', query_block, key_block, precision=highest) * score_scale)
        allowed = inside & (key_ids[None, :] == query_ids[:, None])
        masked = jnp.where(allowed[None], scores, mask_fill)
        row_max = lax.optimization_barrier(jnp.max(masked, axis=-1, keepdims=True))
        unnormed = jnp.exp(masked - row_max)
        attn_probs = low(unnormed / lax.optimization_barrier(jnp.sum(unnormed, axis=-1, keepdims=True)))
        return jnp.einsum('hqk,kd->qhd', attn_probs, value_block, precision=highest)
    starts = jnp.arange(length // QBLK, dtype=jnp.int32) * QBLK
    blocks = lax.map(one_block, starts)
    return blocks.reshape(length, HEADS * HD)

def layer(inputs, doc_rows, w_query, w_key, w_value, w_out, w_gate, w_up, w_down, gain_attn_in, gain_attn_out, gain_ffn_in, gain_ffn_out, gain_query, gain_key):
    length = inputs.shape[0]
    cosine, sine_part = rope_angles(jnp.arange(length, dtype=jnp.int32))
    attn_input = low(rms_scale(inputs, gain_attn_in))
    query_pre = low_back(jnp.dot(attn_input, w_query, precision=highest))
    key_pre = low_back(jnp.dot(attn_input, w_key, precision=highest))
    value_rows = low(low_back(jnp.dot(attn_input, w_value, precision=highest)))
    query_rot = low(rotate(rms_scale(query_pre.reshape(length, HEADS, HD), gain_query), cosine[:, None, :], sine_part[:, None, :]))
    key_rot = low(rotate(rms_scale(key_pre, gain_key), cosine, sine_part))
    heads_out = low(low_back(attend(query_rot, key_rot, value_rows, doc_rows)))
    attn_proj = low_back(jnp.dot(heads_out, w_out, precision=highest))
    middle = inputs + rms_scale(attn_proj, gain_attn_out)
    ffn_input = low(rms_scale(middle, gain_ffn_in))
    gate_pre = low_back(jnp.dot(ffn_input, w_gate, precision=highest))
    up_pre = low_back(jnp.dot(ffn_input, w_up, precision=highest))
    hidden = low(jax.nn.gelu(gate_pre, approximate=True) * up_pre)
    ffn_out = low_back(jnp.dot(hidden, w_down, precision=highest))
    return middle + rms_scale(ffn_out, gain_ffn_out)

def reference(tokens, document_ids, cotangent, w_query, w_key, w_value, w_out, w_gate, w_up, w_down, gain_attn_in, gain_attn_out, gain_ffn_in, gain_ffn_out, gain_query, gain_key):
    params = tuple((item.astype(jnp.float32) for item in (w_query, w_key, w_value, w_out, w_gate, w_up, w_down, gain_attn_in, gain_attn_out, gain_ffn_in, gain_ffn_out, gain_query, gain_key)))

    def group_step(totals, group):
        group_tokens, group_ids, group_cot = group

        def forward(inputs, *weights):
            return layer(inputs, group_ids, *weights)
        result, pull_back = jax.vjp(forward, group_tokens.astype(jnp.float32), *params)
        grads = pull_back(group_cot.astype(jnp.float32))
        totals = tuple((total + grad_part for total, grad_part in zip(totals, grads[1:])))
        return (totals, (result.astype(jnp.bfloat16), grads[0]))
    zeros_init = tuple((jnp.zeros(item.shape, jnp.float32) for item in params))
    totals, (outputs, input_grads) = lax.scan(group_step, zeros_init, (tokens, document_ids, cotangent))
    return (outputs, input_grads, totals[0], totals[1], totals[2], totals[3], totals[4], totals[5], totals[6], totals[7], totals[8], totals[9], totals[10], totals[11], totals[12])
```

```python
import jax
import jax.numpy as jnp
from jax import lax
from jax.sharding import PartitionSpec as P

WINDOW = 512
QBLK = 512


norm_epsilon = 1e-06
rope_base = 10000.0
score_scale = 0.0625
mask_fill = -1e30


def passed_along(value, axis, steps):
    count = lax.axis_size(axis)
    initial, last = (max(0, -steps), min(count, count - steps))
    return lax.ppermute(value, axis, [(source, source + steps) for source in range(initial, last)])


def rms_scale(values, gain_vec):
    return (
        values
        * lax.rsqrt(jnp.mean(values * values, axis=-1, keepdims=True) + norm_epsilon)
        * gain_vec
    )


def rope_angles(positions, head_dim):
    freq_steps = jnp.arange(0, head_dim, 2).astype(jnp.float32) / head_dim
    inverse = jnp.exp(-jnp.log(rope_base) * freq_steps)
    angles = positions.astype(jnp.float32)[:, None] * inverse[None, :]
    return (jnp.cos(angles), jnp.sin(angles))


def rotate(values, cosine, sine_part):
    half_width = values.shape[-1] // 2
    first_half = values[..., :half_width]
    second_half = values[..., half_width:]
    return jnp.concatenate(
        [
            first_half * cosine - second_half * sine_part,
            second_half * cosine + first_half * sine_part,
        ],
        axis=-1,
    )


def gated(gate_in, up_in):
    return jax.nn.gelu(gate_in, approximate=True) * up_in


def contract_rows(left_side, right_side):
    return lax.dot_general(
        left_side, right_side, (((0,), (0,)), ((), ())), preferred_element_type=jnp.float32
    )


def contract_cols(left_side, right_side):
    return lax.dot_general(
        left_side, right_side, (((1,), (1,)), ((), ())), preferred_element_type=jnp.float32
    )


def local_generic(
    tokens,
    document_ids,
    cotangent,
    w_query,
    w_key,
    w_value,
    w_out,
    w_gate,
    w_up,
    w_down,
    gain_attn_in,
    gain_attn_out,
    gain_ffn_in,
    gain_ffn_out,
    gain_query,
    gain_key,
):
    gathered = (
        lax.all_gather(w_query, "fsdp", axis=0, tiled=True),
        lax.all_gather(w_key, "fsdp", axis=0, tiled=True),
        lax.all_gather(w_value, "fsdp", axis=0, tiled=True),
        lax.all_gather(w_out, "fsdp", axis=0, tiled=True),
        lax.all_gather(w_gate, "fsdp", axis=0, tiled=True),
        lax.all_gather(w_up, "fsdp", axis=0, tiled=True),
        lax.all_gather(w_down, "fsdp", axis=0, tiled=True),
        lax.all_gather(gain_attn_in, "fsdp", axis=0, tiled=True),
        lax.all_gather(gain_attn_out, "fsdp", axis=0, tiled=True),
        lax.all_gather(gain_ffn_in, "fsdp", axis=0, tiled=True),
        lax.all_gather(gain_ffn_out, "fsdp", axis=0, tiled=True),
        lax.all_gather(gain_query, "fsdp", axis=0, tiled=True),
        lax.all_gather(gain_key, "fsdp", axis=0, tiled=True),
    )
    query_mat, key_mat, value_mat, out_mat, gate_mat, up_mat, down_mat = (
        gathered[0],
        gathered[1],
        gathered[2],
        gathered[3],
        gathered[4],
        gathered[5],
        gathered[6],
    )
    norm_attn_in = gathered[7].astype(jnp.float32)
    norm_attn_out = gathered[8].astype(jnp.float32)
    norm_ffn_in = gathered[9].astype(jnp.float32)
    norm_ffn_out = gathered[10].astype(jnp.float32)
    norm_query = gathered[11].astype(jnp.float32)
    norm_key = gathered[12].astype(jnp.float32)
    inputs = tokens[0].astype(jnp.float32)
    length = inputs.shape[0]
    head_dim = key_mat.shape[1]
    heads = query_mat.shape[1] // head_dim
    offset = lax.axis_index("seq") * length
    cosine, sine_part = rope_angles(offset + jnp.arange(length, dtype=jnp.int32), head_dim)

    def query_shape(raw_rows, gain_vec):
        return rotate(
            rms_scale(raw_rows.reshape(length, heads, head_dim), gain_vec),
            cosine[:, None, :],
            sine_part[:, None, :],
        )

    def key_shape(raw_rows, gain_vec):
        return rotate(rms_scale(raw_rows, gain_vec), cosine, sine_part)

    attn_normed, pull_attn_in = jax.vjp(rms_scale, inputs, norm_attn_in)
    attn_input = attn_normed.astype(jnp.bfloat16)
    query_pre = jnp.dot(attn_input, query_mat, preferred_element_type=jnp.float32)
    key_pre = jnp.dot(attn_input, key_mat, preferred_element_type=jnp.float32)
    value_rows = jnp.dot(attn_input, value_mat, preferred_element_type=jnp.float32).astype(
        jnp.bfloat16
    )
    query_turned, pull_query = jax.vjp(query_shape, query_pre, norm_query)
    key_turned, pull_key = jax.vjp(key_shape, key_pre, norm_key)
    query_rot = query_turned.astype(jnp.bfloat16)
    key_rot = key_turned.astype(jnp.bfloat16)
    tail_rows = jnp.stack([key_rot[length - WINDOW + 1 :], value_rows[length - WINDOW + 1 :]])
    tail_prev = passed_along(tail_rows, "seq", 1)
    pad_row = jnp.zeros((1, head_dim), jnp.bfloat16)
    key_all = jnp.concatenate([pad_row, tail_prev[0], key_rot], axis=0)
    value_all = jnp.concatenate([pad_row, tail_prev[1], value_rows], axis=0)
    id_row = document_ids[0]
    pad_ids = jnp.concatenate([jnp.full((WINDOW,), -1, jnp.int32), id_row], axis=0)
    key_ids = lax.dynamic_slice_in_dim(pad_ids, offset, length + WINDOW, 0)
    query_ids = lax.dynamic_slice_in_dim(id_row, offset, length, 0)
    offsets = (
        jnp.arange(QBLK + WINDOW, dtype=jnp.int32)[None, :]
        - jnp.arange(QBLK, dtype=jnp.int32)[:, None]
    )
    inside = (offsets >= 1) & (offsets <= WINDOW)
    block_starts = list(range(0, length, QBLK))

    def masked_scores(block_start):
        query_block = query_rot[block_start : block_start + QBLK]
        key_block = key_all[block_start : block_start + QBLK + WINDOW]
        allowed = inside & (
            key_ids[block_start : block_start + QBLK + WINDOW][None, :]
            == query_ids[block_start : block_start + QBLK][:, None]
        )
        scores = (
            jnp.einsum("qhd,kd->hqk", query_block, key_block, preferred_element_type=jnp.float32)
            * score_scale
        )
        return jnp.where(allowed[None], scores, mask_fill)

    log_totals = []
    head_blocks = []
    for block_start in block_starts:
        masked = masked_scores(block_start)
        row_max = jnp.max(masked, axis=-1, keepdims=True)
        unnormed = jnp.exp(masked - row_max)
        row_total = jnp.sum(unnormed, axis=-1, keepdims=True)
        probs_low = (unnormed / row_total).astype(jnp.bfloat16)
        log_totals.append(row_max + jnp.log(row_total))
        head_blocks.append(
            jnp.einsum(
                "hqk,kd->qhd",
                probs_low,
                value_all[block_start : block_start + QBLK + WINDOW],
                preferred_element_type=jnp.float32,
            )
        )
    heads_out = (
        jnp.concatenate(head_blocks, axis=0).reshape(length, heads * head_dim).astype(jnp.bfloat16)
    )
    attn_proj = jnp.dot(heads_out, out_mat, preferred_element_type=jnp.float32)
    attn_normed_out, pull_attn_out = jax.vjp(rms_scale, attn_proj, norm_attn_out)
    middle = inputs + attn_normed_out
    ffn_normed, pull_ffn_in = jax.vjp(rms_scale, middle, norm_ffn_in)
    ffn_input = ffn_normed.astype(jnp.bfloat16)
    gate_pre = jnp.dot(ffn_input, gate_mat, preferred_element_type=jnp.float32)
    up_pre = jnp.dot(ffn_input, up_mat, preferred_element_type=jnp.float32)
    hidden_full, pull_gelu = jax.vjp(gated, gate_pre, up_pre)
    hidden = hidden_full.astype(jnp.bfloat16)
    ffn_out = jnp.dot(hidden, down_mat, preferred_element_type=jnp.float32)
    ffn_normed_out, pull_ffn_out = jax.vjp(rms_scale, ffn_out, norm_ffn_out)
    result = middle + ffn_normed_out
    out_grad = cotangent[0].astype(jnp.float32)
    ffn_out_grad, gain_fo_grad = pull_ffn_out(out_grad)
    ffn_out_low = ffn_out_grad.astype(jnp.bfloat16)
    down_w_grad = contract_rows(hidden, ffn_out_low)
    hidden_grad = contract_cols(ffn_out_low, down_mat)
    gate_grad, up_grad = pull_gelu(hidden_grad)
    gate_low = gate_grad.astype(jnp.bfloat16)
    up_low = up_grad.astype(jnp.bfloat16)
    gate_w_grad = contract_rows(ffn_input, gate_low)
    up_w_grad = contract_rows(ffn_input, up_low)
    ffn_input_grad = contract_cols(gate_low, gate_mat) + contract_cols(up_low, up_mat)
    middle_part, gain_fi_grad = pull_ffn_in(ffn_input_grad)
    middle_grad = out_grad + middle_part
    attn_proj_grad, gain_ao_grad = pull_attn_out(middle_grad)
    proj_low = attn_proj_grad.astype(jnp.bfloat16)
    out_w_grad = contract_rows(heads_out, proj_low)
    heads_grad = (
        contract_cols(proj_low, out_mat).astype(jnp.bfloat16).reshape(length, heads, head_dim)
    )
    key_acc = jnp.zeros((length + WINDOW, head_dim), jnp.float32)
    value_acc = jnp.zeros((length + WINDOW, head_dim), jnp.float32)
    query_grads = []
    for block_index, block_start in enumerate(block_starts):
        masked = masked_scores(block_start)
        attn_probs = jnp.exp(masked - log_totals[block_index])
        probs_low = attn_probs.astype(jnp.bfloat16)
        grad_block = heads_grad[block_start : block_start + QBLK]
        query_block = query_rot[block_start : block_start + QBLK]
        key_block = key_all[block_start : block_start + QBLK + WINDOW]
        value_block = value_all[block_start : block_start + QBLK + WINDOW]
        probs_grad = jnp.einsum(
            "qhd,kd->hqk", grad_block, value_block, preferred_element_type=jnp.float32
        )
        value_acc = value_acc.at[block_start : block_start + QBLK + WINDOW].add(
            jnp.einsum("hqk,qhd->kd", probs_low, grad_block, preferred_element_type=jnp.float32)
        )
        score_grad = attn_probs * (
            probs_grad - jnp.sum(attn_probs * probs_grad, axis=-1, keepdims=True)
        )
        score_low = score_grad.astype(jnp.bfloat16)
        query_grads.append(
            jnp.einsum("hqk,kd->qhd", score_low, key_block, preferred_element_type=jnp.float32)
            * score_scale
        )
        key_acc = key_acc.at[block_start : block_start + QBLK + WINDOW].add(
            jnp.einsum("hqk,qhd->kd", score_low, query_block, preferred_element_type=jnp.float32)
            * score_scale
        )
    tail_grad = jnp.stack([key_acc[1:WINDOW], value_acc[1:WINDOW]])
    tail_next = passed_along(tail_grad.astype(jnp.bfloat16), "seq", -1).astype(tail_grad.dtype)
    key_own = key_acc[WINDOW:].at[length - WINDOW + 1 :].add(tail_next[0])
    value_own = value_acc[WINDOW:].at[length - WINDOW + 1 :].add(tail_next[1])
    value_low = value_own.astype(jnp.bfloat16)
    key_pre_grad, gain_k_grad = pull_key(key_own)
    query_pre_grad, gain_q_grad = pull_query(jnp.concatenate(query_grads, axis=0))
    key_low = key_pre_grad.astype(jnp.bfloat16)
    query_low = query_pre_grad.astype(jnp.bfloat16)
    query_w_grad = contract_rows(attn_input, query_low)
    key_w_grad = contract_rows(attn_input, key_low)
    value_w_grad = contract_rows(attn_input, value_low)
    attn_input_grad = (
        contract_cols(query_low, query_mat)
        + contract_cols(key_low, key_mat)
        + contract_cols(value_low, value_mat)
    )
    input_part, gain_ai_grad = pull_attn_in(attn_input_grad)
    input_grad = middle_grad + input_part
    row_parts = (
        lax.psum_scatter(query_w_grad, "fsdp", scatter_dimension=0, tiled=True),
        lax.psum_scatter(key_w_grad, "fsdp", scatter_dimension=0, tiled=True),
        lax.psum_scatter(value_w_grad, "fsdp", scatter_dimension=0, tiled=True),
        lax.psum_scatter(out_w_grad, "fsdp", scatter_dimension=0, tiled=True),
        lax.psum_scatter(gate_w_grad, "fsdp", scatter_dimension=0, tiled=True),
        lax.psum_scatter(up_w_grad, "fsdp", scatter_dimension=0, tiled=True),
        lax.psum_scatter(down_w_grad, "fsdp", scatter_dimension=0, tiled=True),
        lax.psum_scatter(gain_ai_grad, "fsdp", scatter_dimension=0, tiled=True),
        lax.psum_scatter(gain_ao_grad, "fsdp", scatter_dimension=0, tiled=True),
        lax.psum_scatter(gain_fi_grad, "fsdp", scatter_dimension=0, tiled=True),
        lax.psum_scatter(gain_fo_grad, "fsdp", scatter_dimension=0, tiled=True),
        lax.psum_scatter(gain_q_grad, "fsdp", scatter_dimension=0, tiled=True),
        lax.psum_scatter(gain_k_grad, "fsdp", scatter_dimension=0, tiled=True),
    )
    finals = lax.psum(
        (
            row_parts[0],
            row_parts[1],
            row_parts[2],
            row_parts[3],
            row_parts[4],
            row_parts[5],
            row_parts[6],
            row_parts[7],
            row_parts[8],
            row_parts[9],
            row_parts[10],
            row_parts[11],
            row_parts[12],
        ),
        "seq",
    )
    return (
        result.astype(jnp.bfloat16)[None],
        input_grad[None],
        finals[0],
        finals[1],
        finals[2],
        finals[3],
        finals[4],
        finals[5],
        finals[6],
        finals[7],
        finals[8],
        finals[9],
        finals[10],
        finals[11],
        finals[12],
    )


LANES = 128


def permuted(value, axis, bit):
    count = lax.axis_size(axis)
    return lax.ppermute(value, axis, [(at, at ^ bit) for at in range(count)])


def added(left, right):
    return left.astype(jnp.float32) + right.astype(jnp.float32)


def half_rows(rows):
    return (rows // 2 + 15) // 16 * 16


def chips_gather(first, second):
    ones, twos = [first], [second]
    for bit in (2, 4):
        ones = ones + [permuted(item, "seq", bit) for item in ones]
    for bit in (4, 2):
        twos = twos + [permuted(item, "seq", bit) for item in twos]
    return [
        jnp.concatenate([ones[x + 2 * y], twos[y + 2 * x]], axis=0) for y in (0, 1) for x in (0, 1)
    ]


def line_gather(piece):
    count = lax.axis_size("fsdp")
    place = lax.axis_index("fsdp")
    zeros = (0,) * piece.ndim
    table = jnp.zeros((3 * count - 2,) + piece.shape, piece.dtype)
    table = lax.dynamic_update_slice(table, piece[None], (place + count - 1,) + zeros)
    right, left = piece, piece
    for step in range(1, count):
        right = lax.ppermute(right, "fsdp", [(at, at + 1) for at in range(step - 1, count - 1)])
        left = lax.ppermute(left, "fsdp", [(at, at - 1) for at in range(1, count - step + 1)])
        table = lax.dynamic_update_slice(table, right[None], (place - step + count - 1,) + zeros)
        table = lax.dynamic_update_slice(table, left[None], (place + step + count - 1,) + zeros)
    return table[count - 1 : 2 * count - 1]


def gather_pieces(piece):
    whole = line_gather(piece)
    half = whole.shape[0] // 2
    own = jnp.stack(chips_gather(whole[:half], whole[half:]))
    return jnp.concatenate([own, permuted(own, "seq", 1)], axis=0)


def reduce_pieces(parts):
    count = lax.axis_size("fsdp")
    place = lax.axis_index("fsdp")
    half = count // 2
    mine = added(parts[:4], permuted(parts[4:], "seq", 1)).astype(jnp.bfloat16)
    ones, twos = mine[:, :half], mine[:, half:]
    ones = added(ones[0::2], permuted(ones[1::2], "seq", 2)).astype(jnp.bfloat16)
    twos = added(twos[:2], permuted(twos[2:], "seq", 4)).astype(jnp.bfloat16)
    ones = added(ones[0], permuted(ones[1], "seq", 4)).astype(jnp.bfloat16)
    twos = added(twos[0], permuted(twos[1], "seq", 2)).astype(jnp.bfloat16)
    own = jnp.concatenate([ones, twos], axis=0)

    def at(index):
        return lax.dynamic_index_in_dim(own, index, 0, keepdims=False)

    right, left = None, None
    for step in range(count - 1):
        up = at(jnp.minimum(count - 1 - step + place, count - 1))
        down = at(jnp.maximum(step - (count - 1) + place, 0))
        if right is not None:
            up = added(up, right).astype(jnp.bfloat16)
            down = added(down, left).astype(jnp.bfloat16)
        right = lax.ppermute(up, "fsdp", [(at_, at_ + 1) for at_ in range(min(step, count - 2) + 1)])
        left = lax.ppermute(
            down, "fsdp", [(at_, at_ - 1) for at_ in range(max(count - 1 - step, 1), count)]
        )
    total = added(at(place), right) + left.astype(jnp.float32)
    low = total.astype(jnp.bfloat16)
    cut = half_rows(low.shape[0])
    ours = jnp.stack(chips_gather(low[:cut], low[cut:]))
    return jnp.concatenate([ours, permuted(ours, "seq", 1)], axis=0)


def placed_pieces(rel, own_place):
    return jnp.stack(
        [lax.dynamic_index_in_dim(rel, at ^ own_place, 0, keepdims=False) for at in range(8)]
    )


def to_slabs(rows):
    height, width = rows.shape
    return rows.reshape(height, width // LANES, LANES).transpose(1, 0, 2).reshape(-1, LANES)


def from_slabs(rows, width):
    count = width // LANES
    return rows.reshape(count, -1, LANES).transpose(1, 0, 2).reshape(-1, width)


def totals_of(vector):
    for axis in ("seq", "fsdp"):
        bit = 1
        while bit < lax.axis_size(axis):
            vector = vector + permuted(vector, axis, bit)
            bit *= 2
    return vector

def local_fast(
    tokens,
    document_ids,
    cotangent,
    w_query,
    w_key,
    w_value,
    w_out,
    w_gate,
    w_up,
    w_down,
    gain_attn_in,
    gain_attn_out,
    gain_ffn_in,
    gain_ffn_out,
    gain_query,
    gain_key,
):
    blocks = lax.axis_size("fsdp")
    place = lax.axis_index("fsdp")
    seq_at = lax.axis_index("seq")
    own_place = (seq_at % 2) * 4 + seq_at // 2
    model = w_query.shape[0] * blocks
    shard_d, shard_ff, shard_hd = w_query.shape[0], w_down.shape[0], w_out.shape[0]
    unit = shard_ff // 8
    gains = jnp.concatenate(
        [gain_attn_in, gain_attn_out, gain_ffn_in, gain_ffn_out, gain_query, gain_key]
    ).reshape(-1, LANES)
    gain_rel = gains[None]
    for bit in (1, 2):
        gain_rel = jnp.concatenate([gain_rel, permuted(gain_rel, "fsdp", bit)], axis=0)
    gain_all = jnp.stack(
        [lax.dynamic_index_in_dim(gain_rel, at ^ place, 0, keepdims=False) for at in range(blocks)]
    ).reshape(blocks, -1).astype(jnp.float32)
    norm_attn_in = gain_all[:, :shard_d].reshape(-1)
    norm_attn_out = gain_all[:, shard_d : 2 * shard_d].reshape(-1)
    norm_ffn_in = gain_all[:, 2 * shard_d : 3 * shard_d].reshape(-1)
    norm_ffn_out = gain_all[:, 3 * shard_d : 4 * shard_d].reshape(-1)
    key_part = gain_query.shape[0]
    norm_query = gain_all[:, 4 * shard_d : 4 * shard_d + key_part].reshape(-1)
    norm_key = gain_all[:, 4 * shard_d + key_part :].reshape(-1)

    first_flat = to_slabs(jnp.concatenate([w_query, w_key, w_value], axis=1))
    first_rows = first_flat.shape[0] // 8
    first_piece = lax.dynamic_slice_in_dim(first_flat, seq_at * first_rows, first_rows, 0)
    first_rel = gather_pieces(first_piece)
    seq_order = [(at % 2) * 4 + at // 2 for at in range(8)]
    first_all = jnp.stack(
        [lax.dynamic_index_in_dim(first_rel, at ^ own_place, 0, keepdims=False) for at in seq_order],
        axis=1,
    )
    first_width = w_query.shape[1] + w_key.shape[1] + w_value.shape[1]
    qkv_mat = (
        first_all.reshape(blocks, first_width // LANES, shard_d, LANES)
        .transpose(0, 2, 1, 3)
        .reshape(model, first_width)
    )
    q_wide, k_wide = w_query.shape[1], w_key.shape[1]
    query_mat = qkv_mat[:, :q_wide]
    key_mat = qkv_mat[:, q_wide : q_wide + k_wide]
    value_mat = qkv_mat[:, q_wide + k_wide :]

    def ff_part(weight):
        part = lax.dynamic_index_in_dim(
            weight.reshape(shard_d, blocks, 8, unit), seq_at, 2, keepdims=False
        )
        return to_slabs(part.reshape(shard_d, blocks * unit))

    gate_piece, up_piece = ff_part(w_gate), ff_part(w_up)
    down_piece = to_slabs(lax.dynamic_slice_in_dim(w_down, seq_at * unit, unit, 0))
    out_part = shard_hd // 8
    out_piece = to_slabs(lax.dynamic_slice_in_dim(w_out, seq_at * out_part, out_part, 0))
    n_gate, n_down, n_out = gate_piece.shape[0], down_piece.shape[0], out_piece.shape[0]
    second_rel = gather_pieces(jnp.concatenate([gate_piece, up_piece, down_piece, out_piece]))

    def wide(parts):
        return (
            parts.reshape(8, blocks, 2, shard_d, LANES)
            .transpose(1, 3, 0, 2, 4)
            .reshape(model, 8 * 2 * LANES)
        )

    gate_mat = wide(second_rel[:, :, :n_gate])
    up_mat = wide(second_rel[:, :, n_gate : 2 * n_gate])
    slabs_d = model // LANES
    down_mat = (
        second_rel[:, :, 2 * n_gate : 2 * n_gate + n_down]
        .reshape(8, blocks, slabs_d, unit, LANES)
        .transpose(0, 1, 3, 2, 4)
        .reshape(-1, model)
    )
    out_rel = second_rel[:, :, 2 * n_gate + n_down :]
    out_mat = (
        jnp.stack(
            [lax.dynamic_index_in_dim(out_rel, at ^ own_place, 0, keepdims=False) for at in seq_order],
            axis=1,
        )
        .reshape(blocks, 8, slabs_d, out_part, LANES)
        .transpose(0, 1, 3, 2, 4)
        .reshape(-1, model)
    )
    inputs = tokens[0].astype(jnp.float32)
    length = inputs.shape[0]
    head_dim = key_mat.shape[1]
    heads = query_mat.shape[1] // head_dim
    offset = lax.axis_index("seq") * length
    cosine, sine_part = rope_angles(offset + jnp.arange(length, dtype=jnp.int32), head_dim)

    def query_shape(raw_rows, gain_vec):
        return rotate(
            rms_scale(raw_rows.reshape(length, heads, head_dim), gain_vec),
            cosine[:, None, :],
            sine_part[:, None, :],
        )

    def key_shape(raw_rows, gain_vec):
        return rotate(rms_scale(raw_rows, gain_vec), cosine, sine_part)

    attn_normed, pull_attn_in = jax.vjp(rms_scale, inputs, norm_attn_in)
    attn_input = attn_normed.astype(jnp.bfloat16)
    query_pre = jnp.dot(attn_input, query_mat, preferred_element_type=jnp.float32)
    key_pre = jnp.dot(attn_input, key_mat, preferred_element_type=jnp.float32)
    value_rows = jnp.dot(attn_input, value_mat, preferred_element_type=jnp.float32).astype(
        jnp.bfloat16
    )
    query_turned, pull_query = jax.vjp(query_shape, query_pre, norm_query)
    key_turned, pull_key = jax.vjp(key_shape, key_pre, norm_key)
    query_rot = query_turned.astype(jnp.bfloat16)
    key_rot = key_turned.astype(jnp.bfloat16)
    tail_rows = jnp.stack([key_rot[length - WINDOW :], value_rows[length - WINDOW :]])
    tail_prev = passed_along(tail_rows, "seq", 1)
    key_all = jnp.concatenate([tail_prev[0], key_rot], axis=0)
    value_all = jnp.concatenate([tail_prev[1], value_rows], axis=0)
    id_row = document_ids[0]
    pad_ids = jnp.concatenate([jnp.full((WINDOW,), -1, jnp.int32), id_row], axis=0)
    key_ids = lax.dynamic_slice_in_dim(pad_ids, offset, length + WINDOW, 0)
    query_ids = lax.dynamic_slice_in_dim(id_row, offset, length, 0)
    offsets = (
        jnp.arange(QBLK + WINDOW, dtype=jnp.int32)[None, :]
        - jnp.arange(QBLK, dtype=jnp.int32)[:, None]
    )
    inside = (offsets >= 1) & (offsets <= WINDOW)
    block_starts = list(range(0, length, QBLK))

    def masked_scores(block_start):
        query_block = query_rot[block_start : block_start + QBLK]
        key_block = key_all[block_start : block_start + QBLK + WINDOW]
        allowed = inside & (
            key_ids[block_start : block_start + QBLK + WINDOW][None, :]
            == query_ids[block_start : block_start + QBLK][:, None]
        )
        scores = (
            jnp.einsum("qhd,kd->hqk", query_block, key_block, preferred_element_type=jnp.float32)
            * score_scale
        )
        return jnp.where(allowed[None], scores, mask_fill)

    log_totals = []
    head_blocks = []
    for block_start in block_starts:
        masked = masked_scores(block_start)
        row_max = jnp.max(masked, axis=-1, keepdims=True)
        unnormed = jnp.exp(masked - row_max)
        row_total = jnp.sum(unnormed, axis=-1, keepdims=True)
        probs_low = (unnormed / row_total).astype(jnp.bfloat16)
        log_totals.append(row_max + jnp.log(row_total))
        head_blocks.append(
            jnp.einsum(
                "hqk,kd->qhd",
                probs_low,
                value_all[block_start : block_start + QBLK + WINDOW],
                preferred_element_type=jnp.float32,
            )
        )
    heads_out = (
        jnp.concatenate(head_blocks, axis=0).reshape(length, heads * head_dim).astype(jnp.bfloat16)
    )
    attn_proj = jnp.dot(heads_out, out_mat, preferred_element_type=jnp.float32)
    attn_normed_out, pull_attn_out = jax.vjp(rms_scale, attn_proj, norm_attn_out)
    middle = inputs + attn_normed_out
    ffn_normed, pull_ffn_in = jax.vjp(rms_scale, middle, norm_ffn_in)
    ffn_input = ffn_normed.astype(jnp.bfloat16)
    gate_pre = jnp.dot(ffn_input, gate_mat, preferred_element_type=jnp.float32)
    up_pre = jnp.dot(ffn_input, up_mat, preferred_element_type=jnp.float32)
    hidden_full, pull_gelu = jax.vjp(gated, gate_pre, up_pre)
    hidden = hidden_full.astype(jnp.bfloat16)
    ffn_out = jnp.dot(hidden, down_mat, preferred_element_type=jnp.float32)
    ffn_normed_out, pull_ffn_out = jax.vjp(rms_scale, ffn_out, norm_ffn_out)
    result = middle + ffn_normed_out
    out_grad = cotangent[0].astype(jnp.float32)
    ffn_out_grad, gain_fo_grad = pull_ffn_out(out_grad)
    ffn_out_low = ffn_out_grad.astype(jnp.bfloat16)
    down_w_grad = contract_rows(hidden, ffn_out_low)
    hidden_grad = contract_cols(ffn_out_low, down_mat)
    gate_grad, up_grad = pull_gelu(hidden_grad)
    gate_low = gate_grad.astype(jnp.bfloat16)
    up_low = up_grad.astype(jnp.bfloat16)
    gate_w_grad = contract_rows(ffn_input, gate_low)
    up_w_grad = contract_rows(ffn_input, up_low)
    ffn_input_grad = contract_cols(gate_low, gate_mat) + contract_cols(up_low, up_mat)
    middle_part, gain_fi_grad = pull_ffn_in(ffn_input_grad)
    middle_grad = out_grad + middle_part
    attn_proj_grad, gain_ao_grad = pull_attn_out(middle_grad)
    proj_low = attn_proj_grad.astype(jnp.bfloat16)
    out_w_grad = contract_rows(heads_out, proj_low)
    heads_grad = (
        contract_cols(proj_low, out_mat).astype(jnp.bfloat16).reshape(length, heads, head_dim)
    )
    key_acc = jnp.zeros((length + WINDOW, head_dim), jnp.float32)
    value_acc = jnp.zeros((length + WINDOW, head_dim), jnp.float32)
    query_grads = []
    for block_index, block_start in enumerate(block_starts):
        masked = masked_scores(block_start)
        attn_probs = jnp.exp(masked - log_totals[block_index])
        probs_low = attn_probs.astype(jnp.bfloat16)
        grad_block = heads_grad[block_start : block_start + QBLK]
        query_block = query_rot[block_start : block_start + QBLK]
        key_block = key_all[block_start : block_start + QBLK + WINDOW]
        value_block = value_all[block_start : block_start + QBLK + WINDOW]
        probs_grad = jnp.einsum(
            "qhd,kd->hqk", grad_block, value_block, preferred_element_type=jnp.float32
        )
        value_acc = value_acc.at[block_start : block_start + QBLK + WINDOW].add(
            jnp.einsum("hqk,qhd->kd", probs_low, grad_block, preferred_element_type=jnp.float32)
        )
        score_grad = attn_probs * (
            probs_grad - jnp.sum(attn_probs * probs_grad, axis=-1, keepdims=True)
        )
        score_low = score_grad.astype(jnp.bfloat16)
        query_grads.append(
            jnp.einsum("hqk,kd->qhd", score_low, key_block, preferred_element_type=jnp.float32)
            * score_scale
        )
        key_acc = key_acc.at[block_start : block_start + QBLK + WINDOW].add(
            jnp.einsum("hqk,qhd->kd", score_low, query_block, preferred_element_type=jnp.float32)
            * score_scale
        )
    tail_grad = jnp.stack([key_acc[:WINDOW], value_acc[:WINDOW]])
    tail_next = passed_along(tail_grad.astype(jnp.bfloat16), "seq", -1).astype(tail_grad.dtype)
    key_own = key_acc[WINDOW:].at[length - WINDOW :].add(tail_next[0])
    value_own = value_acc[WINDOW:].at[length - WINDOW :].add(tail_next[1])
    value_low = value_own.astype(jnp.bfloat16)
    key_pre_grad, gain_k_grad = pull_key(key_own)
    query_pre_grad, gain_q_grad = pull_query(jnp.concatenate(query_grads, axis=0))
    key_low = key_pre_grad.astype(jnp.bfloat16)
    query_low = query_pre_grad.astype(jnp.bfloat16)
    query_w_grad = contract_rows(attn_input, query_low)
    key_w_grad = contract_rows(attn_input, key_low)
    value_w_grad = contract_rows(attn_input, value_low)
    attn_input_grad = (
        contract_cols(query_low, query_mat)
        + contract_cols(key_low, key_mat)
        + contract_cols(value_low, value_mat)
    )
    input_part, gain_ai_grad = pull_attn_in(attn_input_grad)
    input_grad = middle_grad + input_part
    def narrow(grad):
        return (
            grad.reshape(blocks, shard_d, 8, 2, LANES)
            .transpose(2, 0, 3, 1, 4)
            .reshape(8, blocks, n_gate, LANES)
            .astype(jnp.bfloat16)
        )

    down_parts = (
        down_w_grad.reshape(8, blocks, unit, slabs_d, LANES)
        .transpose(0, 1, 3, 2, 4)
        .reshape(8, blocks, n_down, LANES)
        .astype(jnp.bfloat16)
    )
    out_abs = (
        out_w_grad.reshape(blocks, 8, out_part, slabs_d, LANES)
        .transpose(1, 0, 3, 2, 4)
        .reshape(8, blocks, n_out, LANES)
        .astype(jnp.bfloat16)
    )

    def seq_to_rel(parts):
        rel = [j ^ own_place for j in range(8)]
        return jnp.stack(
            [
                lax.dynamic_index_in_dim(parts, (p % 4) * 2 + p // 4, 0, keepdims=False)
                for p in rel
            ]
        )

    def rel_to_seq(rel):
        return jnp.stack(
            [lax.dynamic_index_in_dim(rel, at ^ own_place, 0, keepdims=False) for at in seq_order]
        )

    second_parts = jnp.concatenate(
        [narrow(gate_w_grad), narrow(up_w_grad), down_parts, seq_to_rel(out_abs)], axis=2
    )
    second_final = rel_to_seq(reduce_pieces(second_parts)).astype(jnp.float32)
    first_grad = jnp.concatenate([query_w_grad, key_w_grad, value_w_grad], axis=1)
    first_parts = (
        first_grad.reshape(blocks, shard_d, first_width // LANES, LANES)
        .transpose(0, 2, 1, 3)
        .reshape(blocks, 8, first_rows, LANES)
        .transpose(1, 0, 2, 3)
        .astype(jnp.bfloat16)
    )
    first_final = rel_to_seq(reduce_pieces(seq_to_rel(first_parts))).astype(jnp.float32)
    first_own = from_slabs(first_final.reshape(-1, LANES), first_width)

    def ff_own(parts):
        return (
            parts.reshape(8, 2, shard_d, LANES)
            .transpose(2, 0, 1, 3)
            .reshape(shard_d, 8, blocks, unit)
            .transpose(0, 2, 1, 3)
            .reshape(shard_d, -1)
        )

    def row_own(parts, height):
        return parts.reshape(8, slabs_d, height, LANES).transpose(0, 2, 1, 3).reshape(-1, model)

    gain_sum = totals_of(
        jnp.concatenate(
            [gain_ai_grad, gain_ao_grad, gain_fi_grad, gain_fo_grad, gain_q_grad, gain_k_grad]
        ).reshape(-1, LANES)
    ).reshape(-1)

    def gain_own(start, size):
        return lax.dynamic_slice_in_dim(gain_sum, start + place * size, size, 0)

    finals = (
        first_own[:, :q_wide],
        first_own[:, q_wide : q_wide + k_wide],
        first_own[:, q_wide + k_wide :],
        row_own(second_final[:, 2 * n_gate + n_down :], out_part),
        ff_own(second_final[:, :n_gate]),
        ff_own(second_final[:, n_gate : 2 * n_gate]),
        row_own(second_final[:, 2 * n_gate : 2 * n_gate + n_down], unit),
        gain_own(0, shard_d),
        gain_own(model, shard_d),
        gain_own(2 * model, shard_d),
        gain_own(3 * model, shard_d),
        gain_own(4 * model, key_part),
        gain_own(4 * model + head_dim, key_part),
    )
    return (
        result.astype(jnp.bfloat16)[None],
        input_grad[None],
        finals[0],
        finals[1],
        finals[2],
        finals[3],
        finals[4],
        finals[5],
        finals[6],
        finals[7],
        finals[8],
        finals[9],
        finals[10],
        finals[11],
        finals[12],
    )


def solution(mesh):
    fits = mesh.shape["seq"] == 8 and mesh.shape["fsdp"] == 4
    placed = (
        P("fsdp", "seq", None),
        P("fsdp", None),
        P("fsdp", "seq", None),
        P("fsdp", None),
        P("fsdp", None),
        P("fsdp", None),
        P("fsdp", None),
        P("fsdp", None),
        P("fsdp", None),
        P("fsdp", None),
        P("fsdp"),
        P("fsdp"),
        P("fsdp"),
        P("fsdp"),
        P("fsdp"),
        P("fsdp"),
    )
    return jax.shard_map(
        local_fast if fits else local_generic,
        mesh=mesh,
        in_specs=placed,
        out_specs=(
            P("fsdp", "seq", None),
            P("fsdp", "seq", None),
            P("fsdp", None),
            P("fsdp", None),
            P("fsdp", None),
            P("fsdp", None),
            P("fsdp", None),
            P("fsdp", None),
            P("fsdp", None),
            P("fsdp"),
            P("fsdp"),
            P("fsdp"),
            P("fsdp"),
            P("fsdp"),
            P("fsdp"),
        ),
        check_vma=False,
    )
```

```python
import jax
import jax.numpy as jnp
from jax import lax
from jax.experimental import pallas as pl
from jax.experimental.pallas import tpu as pltpu
from jax.sharding import PartitionSpec as P

WINDOW = 512
QBLK = 512


norm_epsilon = 1e-06
rope_base = 10000.0
score_scale = 0.0625
mask_fill = -1e30


def passed_along(value, axis, steps):
    count = lax.axis_size(axis)
    initial, last = (max(0, -steps), min(count, count - steps))
    return lax.ppermute(value, axis, [(source, source + steps) for source in range(initial, last)])


def rms_scale(values, gain_vec):
    return (
        values
        * lax.rsqrt(jnp.mean(values * values, axis=-1, keepdims=True) + norm_epsilon)
        * gain_vec
    )


def rope_angles(positions, head_dim):
    freq_steps = jnp.arange(0, head_dim, 2).astype(jnp.float32) / head_dim
    inverse = jnp.exp(-jnp.log(rope_base) * freq_steps)
    angles = positions.astype(jnp.float32)[:, None] * inverse[None, :]
    return (jnp.cos(angles), jnp.sin(angles))


def rotate(values, cosine, sine_part):
    half_width = values.shape[-1] // 2
    first_half = values[..., :half_width]
    second_half = values[..., half_width:]
    return jnp.concatenate(
        [
            first_half * cosine - second_half * sine_part,
            second_half * cosine + first_half * sine_part,
        ],
        axis=-1,
    )


def gated(gate_in, up_in):
    return jax.nn.gelu(gate_in, approximate=True) * up_in


def contract_rows(left_side, right_side):
    return lax.dot_general(
        left_side, right_side, (((0,), (0,)), ((), ())), preferred_element_type=jnp.float32
    )


def contract_cols(left_side, right_side):
    return lax.dot_general(
        left_side, right_side, (((1,), (1,)), ((), ())), preferred_element_type=jnp.float32
    )


def local_generic(
    tokens,
    document_ids,
    cotangent,
    w_query,
    w_key,
    w_value,
    w_out,
    w_gate,
    w_up,
    w_down,
    gain_attn_in,
    gain_attn_out,
    gain_ffn_in,
    gain_ffn_out,
    gain_query,
    gain_key,
):
    gathered = (
        lax.all_gather(w_query, "fsdp", axis=0, tiled=True),
        lax.all_gather(w_key, "fsdp", axis=0, tiled=True),
        lax.all_gather(w_value, "fsdp", axis=0, tiled=True),
        lax.all_gather(w_out, "fsdp", axis=0, tiled=True),
        lax.all_gather(w_gate, "fsdp", axis=0, tiled=True),
        lax.all_gather(w_up, "fsdp", axis=0, tiled=True),
        lax.all_gather(w_down, "fsdp", axis=0, tiled=True),
        lax.all_gather(gain_attn_in, "fsdp", axis=0, tiled=True),
        lax.all_gather(gain_attn_out, "fsdp", axis=0, tiled=True),
        lax.all_gather(gain_ffn_in, "fsdp", axis=0, tiled=True),
        lax.all_gather(gain_ffn_out, "fsdp", axis=0, tiled=True),
        lax.all_gather(gain_query, "fsdp", axis=0, tiled=True),
        lax.all_gather(gain_key, "fsdp", axis=0, tiled=True),
    )
    query_mat, key_mat, value_mat, out_mat, gate_mat, up_mat, down_mat = (
        gathered[0],
        gathered[1],
        gathered[2],
        gathered[3],
        gathered[4],
        gathered[5],
        gathered[6],
    )
    norm_attn_in = gathered[7].astype(jnp.float32)
    norm_attn_out = gathered[8].astype(jnp.float32)
    norm_ffn_in = gathered[9].astype(jnp.float32)
    norm_ffn_out = gathered[10].astype(jnp.float32)
    norm_query = gathered[11].astype(jnp.float32)
    norm_key = gathered[12].astype(jnp.float32)
    inputs = tokens[0].astype(jnp.float32)
    length = inputs.shape[0]
    head_dim = key_mat.shape[1]
    heads = query_mat.shape[1] // head_dim
    offset = lax.axis_index("seq") * length
    cosine, sine_part = rope_angles(offset + jnp.arange(length, dtype=jnp.int32), head_dim)

    def query_shape(raw_rows, gain_vec):
        return rotate(
            rms_scale(raw_rows.reshape(length, heads, head_dim), gain_vec),
            cosine[:, None, :],
            sine_part[:, None, :],
        )

    def key_shape(raw_rows, gain_vec):
        return rotate(rms_scale(raw_rows, gain_vec), cosine, sine_part)

    attn_normed, pull_attn_in = jax.vjp(rms_scale, inputs, norm_attn_in)
    attn_input = attn_normed.astype(jnp.bfloat16)
    query_pre = jnp.dot(attn_input, query_mat, preferred_element_type=jnp.float32)
    key_pre = jnp.dot(attn_input, key_mat, preferred_element_type=jnp.float32)
    value_rows = jnp.dot(attn_input, value_mat, preferred_element_type=jnp.float32).astype(
        jnp.bfloat16
    )
    query_turned, pull_query = jax.vjp(query_shape, query_pre, norm_query)
    key_turned, pull_key = jax.vjp(key_shape, key_pre, norm_key)
    query_rot = query_turned.astype(jnp.bfloat16)
    key_rot = key_turned.astype(jnp.bfloat16)
    tail_rows = jnp.stack([key_rot[length - WINDOW + 1 :], value_rows[length - WINDOW + 1 :]])
    tail_prev = passed_along(tail_rows, "seq", 1)
    pad_row = jnp.zeros((1, head_dim), jnp.bfloat16)
    key_all = jnp.concatenate([pad_row, tail_prev[0], key_rot], axis=0)
    value_all = jnp.concatenate([pad_row, tail_prev[1], value_rows], axis=0)
    id_row = document_ids[0]
    pad_ids = jnp.concatenate([jnp.full((WINDOW,), -1, jnp.int32), id_row], axis=0)
    key_ids = lax.dynamic_slice_in_dim(pad_ids, offset, length + WINDOW, 0)
    query_ids = lax.dynamic_slice_in_dim(id_row, offset, length, 0)
    offsets = (
        jnp.arange(QBLK + WINDOW, dtype=jnp.int32)[None, :]
        - jnp.arange(QBLK, dtype=jnp.int32)[:, None]
    )
    inside = (offsets >= 1) & (offsets <= WINDOW)
    block_starts = list(range(0, length, QBLK))

    def masked_scores(block_start):
        query_block = query_rot[block_start : block_start + QBLK]
        key_block = key_all[block_start : block_start + QBLK + WINDOW]
        allowed = inside & (
            key_ids[block_start : block_start + QBLK + WINDOW][None, :]
            == query_ids[block_start : block_start + QBLK][:, None]
        )
        scores = (
            jnp.einsum("qhd,kd->hqk", query_block, key_block, preferred_element_type=jnp.float32)
            * score_scale
        )
        return jnp.where(allowed[None], scores, mask_fill)

    log_totals = []
    head_blocks = []
    for block_start in block_starts:
        masked = masked_scores(block_start)
        row_max = jnp.max(masked, axis=-1, keepdims=True)
        unnormed = jnp.exp(masked - row_max)
        row_total = jnp.sum(unnormed, axis=-1, keepdims=True)
        probs_low = (unnormed / row_total).astype(jnp.bfloat16)
        log_totals.append(row_max + jnp.log(row_total))
        head_blocks.append(
            jnp.einsum(
                "hqk,kd->qhd",
                probs_low,
                value_all[block_start : block_start + QBLK + WINDOW],
                preferred_element_type=jnp.float32,
            )
        )
    heads_out = (
        jnp.concatenate(head_blocks, axis=0).reshape(length, heads * head_dim).astype(jnp.bfloat16)
    )
    attn_proj = jnp.dot(heads_out, out_mat, preferred_element_type=jnp.float32)
    attn_normed_out, pull_attn_out = jax.vjp(rms_scale, attn_proj, norm_attn_out)
    middle = inputs + attn_normed_out
    ffn_normed, pull_ffn_in = jax.vjp(rms_scale, middle, norm_ffn_in)
    ffn_input = ffn_normed.astype(jnp.bfloat16)
    gate_pre = jnp.dot(ffn_input, gate_mat, preferred_element_type=jnp.float32)
    up_pre = jnp.dot(ffn_input, up_mat, preferred_element_type=jnp.float32)
    hidden_full, pull_gelu = jax.vjp(gated, gate_pre, up_pre)
    hidden = hidden_full.astype(jnp.bfloat16)
    ffn_out = jnp.dot(hidden, down_mat, preferred_element_type=jnp.float32)
    ffn_normed_out, pull_ffn_out = jax.vjp(rms_scale, ffn_out, norm_ffn_out)
    result = middle + ffn_normed_out
    out_grad = cotangent[0].astype(jnp.float32)
    ffn_out_grad, gain_fo_grad = pull_ffn_out(out_grad)
    ffn_out_low = ffn_out_grad.astype(jnp.bfloat16)
    down_w_grad = contract_rows(hidden, ffn_out_low)
    hidden_grad = contract_cols(ffn_out_low, down_mat)
    gate_grad, up_grad = pull_gelu(hidden_grad)
    gate_low = gate_grad.astype(jnp.bfloat16)
    up_low = up_grad.astype(jnp.bfloat16)
    gate_w_grad = contract_rows(ffn_input, gate_low)
    up_w_grad = contract_rows(ffn_input, up_low)
    ffn_input_grad = contract_cols(gate_low, gate_mat) + contract_cols(up_low, up_mat)
    middle_part, gain_fi_grad = pull_ffn_in(ffn_input_grad)
    middle_grad = out_grad + middle_part
    attn_proj_grad, gain_ao_grad = pull_attn_out(middle_grad)
    proj_low = attn_proj_grad.astype(jnp.bfloat16)
    out_w_grad = contract_rows(heads_out, proj_low)
    heads_grad = (
        contract_cols(proj_low, out_mat).astype(jnp.bfloat16).reshape(length, heads, head_dim)
    )
    key_acc = jnp.zeros((length + WINDOW, head_dim), jnp.float32)
    value_acc = jnp.zeros((length + WINDOW, head_dim), jnp.float32)
    query_grads = []
    for block_index, block_start in enumerate(block_starts):
        masked = masked_scores(block_start)
        attn_probs = jnp.exp(masked - log_totals[block_index])
        probs_low = attn_probs.astype(jnp.bfloat16)
        grad_block = heads_grad[block_start : block_start + QBLK]
        query_block = query_rot[block_start : block_start + QBLK]
        key_block = key_all[block_start : block_start + QBLK + WINDOW]
        value_block = value_all[block_start : block_start + QBLK + WINDOW]
        probs_grad = jnp.einsum(
            "qhd,kd->hqk", grad_block, value_block, preferred_element_type=jnp.float32
        )
        value_acc = value_acc.at[block_start : block_start + QBLK + WINDOW].add(
            jnp.einsum("hqk,qhd->kd", probs_low, grad_block, preferred_element_type=jnp.float32)
        )
        score_grad = attn_probs * (
            probs_grad - jnp.sum(attn_probs * probs_grad, axis=-1, keepdims=True)
        )
        score_low = score_grad.astype(jnp.bfloat16)
        query_grads.append(
            jnp.einsum("hqk,kd->qhd", score_low, key_block, preferred_element_type=jnp.float32)
            * score_scale
        )
        key_acc = key_acc.at[block_start : block_start + QBLK + WINDOW].add(
            jnp.einsum("hqk,qhd->kd", score_low, query_block, preferred_element_type=jnp.float32)
            * score_scale
        )
    tail_grad = jnp.stack([key_acc[1:WINDOW], value_acc[1:WINDOW]])
    tail_next = passed_along(tail_grad.astype(jnp.bfloat16), "seq", -1).astype(tail_grad.dtype)
    key_own = key_acc[WINDOW:].at[length - WINDOW + 1 :].add(tail_next[0])
    value_own = value_acc[WINDOW:].at[length - WINDOW + 1 :].add(tail_next[1])
    value_low = value_own.astype(jnp.bfloat16)
    key_pre_grad, gain_k_grad = pull_key(key_own)
    query_pre_grad, gain_q_grad = pull_query(jnp.concatenate(query_grads, axis=0))
    key_low = key_pre_grad.astype(jnp.bfloat16)
    query_low = query_pre_grad.astype(jnp.bfloat16)
    query_w_grad = contract_rows(attn_input, query_low)
    key_w_grad = contract_rows(attn_input, key_low)
    value_w_grad = contract_rows(attn_input, value_low)
    attn_input_grad = (
        contract_cols(query_low, query_mat)
        + contract_cols(key_low, key_mat)
        + contract_cols(value_low, value_mat)
    )
    input_part, gain_ai_grad = pull_attn_in(attn_input_grad)
    input_grad = middle_grad + input_part
    row_parts = (
        lax.psum_scatter(query_w_grad, "fsdp", scatter_dimension=0, tiled=True),
        lax.psum_scatter(key_w_grad, "fsdp", scatter_dimension=0, tiled=True),
        lax.psum_scatter(value_w_grad, "fsdp", scatter_dimension=0, tiled=True),
        lax.psum_scatter(out_w_grad, "fsdp", scatter_dimension=0, tiled=True),
        lax.psum_scatter(gate_w_grad, "fsdp", scatter_dimension=0, tiled=True),
        lax.psum_scatter(up_w_grad, "fsdp", scatter_dimension=0, tiled=True),
        lax.psum_scatter(down_w_grad, "fsdp", scatter_dimension=0, tiled=True),
        lax.psum_scatter(gain_ai_grad, "fsdp", scatter_dimension=0, tiled=True),
        lax.psum_scatter(gain_ao_grad, "fsdp", scatter_dimension=0, tiled=True),
        lax.psum_scatter(gain_fi_grad, "fsdp", scatter_dimension=0, tiled=True),
        lax.psum_scatter(gain_fo_grad, "fsdp", scatter_dimension=0, tiled=True),
        lax.psum_scatter(gain_q_grad, "fsdp", scatter_dimension=0, tiled=True),
        lax.psum_scatter(gain_k_grad, "fsdp", scatter_dimension=0, tiled=True),
    )
    finals = lax.psum(
        (
            row_parts[0],
            row_parts[1],
            row_parts[2],
            row_parts[3],
            row_parts[4],
            row_parts[5],
            row_parts[6],
            row_parts[7],
            row_parts[8],
            row_parts[9],
            row_parts[10],
            row_parts[11],
            row_parts[12],
        ),
        "seq",
    )
    return (
        result.astype(jnp.bfloat16)[None],
        input_grad[None],
        finals[0],
        finals[1],
        finals[2],
        finals[3],
        finals[4],
        finals[5],
        finals[6],
        finals[7],
        finals[8],
        finals[9],
        finals[10],
        finals[11],
        finals[12],
    )


LANES = 128


def permuted(value, axis, bit):
    count = lax.axis_size(axis)
    return lax.ppermute(value, axis, [(at, at ^ bit) for at in range(count)])


def added(left, right):
    return left.astype(jnp.float32) + right.astype(jnp.float32)


def half_rows(rows):
    return (rows // 2 + 15) // 16 * 16


def chips_gather(first, second):
    ones, twos = [first], [second]
    for bit in (2, 4):
        ones = ones + [permuted(item, "seq", bit) for item in ones]
    for bit in (4, 2):
        twos = twos + [permuted(item, "seq", bit) for item in twos]
    return [
        jnp.concatenate([ones[x + 2 * y], twos[y + 2 * x]], axis=0) for y in (0, 1) for x in (0, 1)
    ]


def line_gather(piece):
    count = lax.axis_size("fsdp")
    place = lax.axis_index("fsdp")
    zeros = (0,) * piece.ndim
    table = jnp.zeros((3 * count - 2,) + piece.shape, piece.dtype)
    table = lax.dynamic_update_slice(table, piece[None], (place + count - 1,) + zeros)
    right, left = piece, piece
    for step in range(1, count):
        right = lax.ppermute(right, "fsdp", [(at, at + 1) for at in range(step - 1, count - 1)])
        left = lax.ppermute(left, "fsdp", [(at, at - 1) for at in range(1, count - step + 1)])
        table = lax.dynamic_update_slice(table, right[None], (place - step + count - 1,) + zeros)
        table = lax.dynamic_update_slice(table, left[None], (place + step + count - 1,) + zeros)
    return table[count - 1 : 2 * count - 1]


def after(value, *others):
    return lax.optimization_barrier((value,) + others)[0]


def pair_gather(piece):
    count = lax.axis_size("fsdp")
    place = lax.axis_index("fsdp")
    rel, bit = piece[None], 1
    while bit < count:
        rel = jnp.concatenate([rel, permuted(rel, "fsdp", bit)], axis=0)
        bit *= 2
    return jnp.stack(
        [lax.dynamic_index_in_dim(rel, at ^ place, 0, keepdims=False) for at in range(count)]
    )


def pair_reduce(own):
    place = lax.axis_index("fsdp")
    bit = lax.axis_size("fsdp") // 2
    while bit:
        mine = (place // bit) % 2
        halves = own.reshape((2, bit) + own.shape[1:])
        sent = lax.dynamic_index_in_dim(halves, 1 - mine, 0, keepdims=False)
        kept = lax.dynamic_index_in_dim(halves, mine, 0, keepdims=False)
        total = added(kept, permuted(sent, "fsdp", bit))
        own = total.astype(jnp.bfloat16)
        bit //= 2
    return total[0]


def line_reduce(own):
    count = lax.axis_size("fsdp")
    place = lax.axis_index("fsdp")

    def at(index):
        return lax.dynamic_index_in_dim(own, index, 0, keepdims=False)

    right, left = None, None
    for step in range(count - 1):
        up = at(jnp.minimum(count - 1 - step + place, count - 1))
        down = at(jnp.maximum(step - (count - 1) + place, 0))
        if right is not None:
            up = added(up, right).astype(jnp.bfloat16)
            down = added(down, left).astype(jnp.bfloat16)
        right = lax.ppermute(up, "fsdp", [(at_, at_ + 1) for at_ in range(min(step, count - 2) + 1)])
        left = lax.ppermute(
            down, "fsdp", [(at_, at_ - 1) for at_ in range(max(count - 1 - step, 1), count)]
        )
    return added(at(place), right) + left.astype(jnp.float32)


def gather_stages(piece, along):
    whole = along(piece)
    yield whole
    half = whole.shape[0] // 2
    first, second = whole[:half], whole[half:]
    own = jnp.stack(chips_gather(first, second))
    yield own
    yield jnp.concatenate([own, permuted(own, "seq", 1)], axis=0)


def reduce_stages(parts, along):
    half = parts.shape[1] // 2
    mine = added(parts[:4], permuted(parts[4:], "seq", 1)).astype(jnp.bfloat16)
    yield mine
    ones, twos = mine[:, :half], mine[:, half:]
    ones = added(ones[0::2], permuted(ones[1::2], "seq", 2)).astype(jnp.bfloat16)
    twos = added(twos[:2], permuted(twos[2:], "seq", 4)).astype(jnp.bfloat16)
    yield (ones, twos)
    ones = added(ones[0], permuted(ones[1], "seq", 4)).astype(jnp.bfloat16)
    twos = added(twos[0], permuted(twos[1], "seq", 2)).astype(jnp.bfloat16)
    own = jnp.concatenate([ones, twos], axis=0)
    yield own
    low = along(own).astype(jnp.bfloat16)
    cut = half_rows(low.shape[0])
    ours = jnp.stack(chips_gather(low[:cut], low[cut:]))
    yield jnp.concatenate([ours, permuted(ours, "seq", 1)], axis=0)


def to_slabs(rows):
    height, width = rows.shape
    return rows.reshape(height, width // LANES, LANES).transpose(1, 0, 2).reshape(-1, LANES)


def from_slabs(rows, width):
    count = width // LANES
    return rows.reshape(count, -1, LANES).transpose(1, 0, 2).reshape(-1, width)


def totals_of(vector):
    for axis in ("seq", "fsdp"):
        bit = 1
        while bit < lax.axis_size(axis):
            vector = vector + permuted(vector, axis, bit)
            bit *= 2
    return vector

TOK_BLK = 256
gelu_scale = 0.7978845608028654
gelu_cubic = 0.044715


def dot_cols(left_side, right_side):
    return lax.dot_general(
        left_side, right_side, (((1,), (1,)), ((), ())), preferred_element_type=jnp.float32
    )


def dot_plain(left_side, right_side):
    return jnp.dot(left_side, right_side, preferred_element_type=jnp.float32)


def row_rate(rows):
    return lax.rsqrt(jnp.mean(rows * rows, axis=-1, keepdims=True) + norm_epsilon)


def norm_back(rows, gain_row, grad):
    rate = row_rate(rows)
    scaled = gain_row * grad
    back = rate * scaled - rows * (
        rate * rate * rate * jnp.mean(rows * scaled, axis=-1, keepdims=True)
    )
    return back, jnp.sum(rows * rate * grad, axis=0, keepdims=True)


def middle_kernel(
    heads_ref,
    tok_ref,
    cot_ref,
    gain_ref,
    out_w_ref,
    pack_ref,
    result_ref,
    mid_grad_ref,
    heads_grad_ref,
    out_grad_ref,
    gain_grad_ref,
    pack_grad_ref,
    proj_sc,
    mid_sc,
    norm_sc,
    turn_sc,
    gate_sc,
    up_sc,
    acc_sc,
    back_sc,
    gate_low_sc,
    up_low_sc,
    hid_low_sc,
    gate_w_sc,
    up_w_sc,
    down_w_sc,
):
    step = pl.program_id(0)
    blocks, _, lanes = pack_ref.shape[1:]
    length, model = tok_ref.shape
    part_d = model // blocks
    wide = gate_w_sc.shape[1] // lanes
    slabs = model // lanes
    unit = gate_w_sc.shape[1] // blocks
    rows_g = wide * part_d
    chunks = gate_sc.shape[0]
    chunk = lax.rem(step, chunks)

    for block in range(blocks):
        for slab in range(wide):
            take = slice(slab * part_d, (slab + 1) * part_d)
            also = slice(rows_g + slab * part_d, rows_g + (slab + 1) * part_d)
            into = slice(block * part_d, (block + 1) * part_d)
            lane = slice(slab * lanes, (slab + 1) * lanes)
            gate_w_sc[into, lane] = pack_ref[0, block, take, :]
            up_w_sc[into, lane] = pack_ref[0, block, also, :]
        for slab in range(slabs):
            take = slice(2 * rows_g + slab * unit, 2 * rows_g + (slab + 1) * unit)
            down_w_sc[block * unit : (block + 1) * unit, slab * lanes : (slab + 1) * lanes] = (
                pack_ref[0, block, take, :]
            )

    gain_ao, gain_fi, gain_fo = gain_ref[0:1], gain_ref[1:2], gain_ref[2:3]

    def each(body):
        def wrapped(at, carry):
            body(pl.ds(pl.multiple_of(at * TOK_BLK, TOK_BLK), TOK_BLK))
            return carry

        lax.fori_loop(0, length // TOK_BLK, wrapped, 0)

    @pl.when(step == 0)
    def _():
        gain_grad_ref[...] = jnp.zeros_like(gain_grad_ref)

        def start(rows):
            proj = dot_plain(heads_ref[rows, :], out_w_ref[...])
            proj_sc[rows, :] = proj
            middle = tok_ref[rows, :].astype(jnp.float32) + proj * row_rate(proj) * gain_ao
            mid_sc[rows, :] = middle
            norm_sc[rows, :] = (middle * row_rate(middle) * gain_fi).astype(jnp.bfloat16)
            acc_sc[rows, :] = jnp.zeros((TOK_BLK, model), jnp.float32)

        each(start)
        for at in range(length // TOK_BLK):
            rows = slice(at * TOK_BLK, (at + 1) * TOK_BLK)
            turn_sc[:, rows] = norm_sc[rows, :].T

    @pl.when(step < chunks)
    def _():
        def forward(rows):
            gate = dot_plain(norm_sc[rows, :], gate_w_sc[...])
            up = dot_plain(norm_sc[rows, :], up_w_sc[...])
            gate_sc[chunk, rows, :] = gate
            up_sc[chunk, rows, :] = up
            inner = jnp.tanh(gelu_scale * (gate + gelu_cubic * (gate * gate * gate)))
            hidden = (0.5 * gate * (1.0 + inner) * up).astype(jnp.bfloat16)
            acc_sc[rows, :] += dot_plain(hidden, down_w_sc[...])

        each(forward)

    @pl.when(step == chunks)
    def _():
        def turn(rows):
            ffn = acc_sc[rows, :]
            result_ref[rows, :] = (mid_sc[rows, :] + ffn * row_rate(ffn) * gain_fo).astype(
                jnp.bfloat16
            )
            back, gain_part = norm_back(ffn, gain_fo, cot_ref[rows, :].astype(jnp.float32))
            back_sc[rows, :] = back.astype(jnp.bfloat16)
            gain_grad_ref[2:3, :] += gain_part
            acc_sc[rows, :] = jnp.zeros((TOK_BLK, model), jnp.float32)

        each(turn)

    @pl.when(step >= chunks)
    def _():
        def backward(rows):
            gate = gate_sc[chunk, rows, :]
            up = up_sc[chunk, rows, :]
            square = gate * gate
            inner = jnp.tanh(gelu_scale * (gate + gelu_cubic * (square * gate)))
            half = 0.5 * (1.0 + inner)
            active = gate * half
            slope = half + (0.5 * gelu_scale) * gate * (1.0 - inner * inner) * (
                1.0 + 3.0 * gelu_cubic * square
            )
            hid_grad = dot_cols(back_sc[rows, :], down_w_sc[...])
            gate_low = (hid_grad * up * slope).astype(jnp.bfloat16)
            up_low = (hid_grad * active).astype(jnp.bfloat16)
            gate_low_sc[rows, :] = gate_low
            up_low_sc[rows, :] = up_low
            hid_low_sc[rows, :] = (active * up).astype(jnp.bfloat16)
            acc_sc[rows, :] += dot_cols(gate_low, gate_w_sc[...]) + dot_cols(
                up_low, up_w_sc[...]
            )

        each(backward)
        gate_grad = dot_plain(turn_sc[...], gate_low_sc[...]).astype(jnp.bfloat16)
        up_grad = dot_plain(turn_sc[...], up_low_sc[...]).astype(jnp.bfloat16)
        for block in range(blocks):
            for slab in range(wide):
                take = slice(slab * part_d, (slab + 1) * part_d)
                also = slice(rows_g + slab * part_d, rows_g + (slab + 1) * part_d)
                into = slice(block * part_d, (block + 1) * part_d)
                lane = slice(slab * lanes, (slab + 1) * lanes)
                pack_grad_ref[0, block, take, :] = gate_grad[into, lane]
                pack_grad_ref[0, block, also, :] = up_grad[into, lane]
        down_grad = lax.dot_general(
            hid_low_sc[...], back_sc[...], (((0,), (0,)), ((), ())),
            preferred_element_type=jnp.float32,
        ).astype(jnp.bfloat16)
        for block in range(blocks):
            for slab in range(slabs):
                take = slice(2 * rows_g + slab * unit, 2 * rows_g + (slab + 1) * unit)
                pack_grad_ref[0, block, take, :] = down_grad[
                    block * unit : (block + 1) * unit, slab * lanes : (slab + 1) * lanes
                ]

    @pl.when(step == 2 * chunks - 1)
    def _():
        def finish(rows):
            middle = mid_sc[rows, :]
            part, gain_part = norm_back(middle, gain_fi, acc_sc[rows, :])
            gain_grad_ref[1:2, :] += gain_part
            mid_grad = cot_ref[rows, :].astype(jnp.float32) + part
            mid_grad_ref[rows, :] = mid_grad
            proj_grad, gain_part = norm_back(proj_sc[rows, :], gain_ao, mid_grad)
            gain_grad_ref[0:1, :] += gain_part
            low = proj_grad.astype(jnp.bfloat16)
            norm_sc[rows, :] = low
            heads_grad_ref[rows, :] = dot_cols(low, out_w_ref[...]).astype(jnp.bfloat16)

        each(finish)
        share = heads_ref.shape[1] // blocks
        out_rows = out_grad_ref.shape[2] // slabs
        for block in range(blocks):
            grad = lax.dot_general(
                heads_ref[:, block * share : (block + 1) * share], norm_sc[...],
                (((0,), (0,)), ((), ())),
                preferred_element_type=jnp.float32,
            ).astype(jnp.bfloat16)
            for at in range(out_grad_ref.shape[0]):
                for slab in range(slabs):
                    out_grad_ref[at, block, slab * out_rows : (slab + 1) * out_rows, :] = grad[
                        at * out_rows : (at + 1) * out_rows, slab * lanes : (slab + 1) * lanes
                    ]


def middle_layer(heads_out, tokens, cotangent, gains, out_mat, pack, n_gate, n_down, n_out):
    length, model = tokens.shape
    chunks, blocks, rows, lanes = pack.shape
    used = 2 * n_gate + n_down
    width = n_gate * blocks * lanes // model
    total = heads_out.shape[1]

    def still(shape):
        return pl.BlockSpec(
            shape, lambda step: (0,) * len(shape), pipeline_mode=pl.Buffered(1)
        )

    tile = (length, model)
    return pl.pallas_call(
        middle_kernel,
        grid=(2 * chunks,),
        in_specs=[
            still((length, total)),
            still(tile),
            still(tile),
            still(gains.shape),
            still(out_mat.shape),
            pl.BlockSpec((1, blocks, rows, lanes), lambda step: (lax.rem(step, chunks), 0, 0, 0)),
        ],
        out_specs=[
            still(tile),
            still(tile),
            still((length, total)),
            still((chunks, blocks, n_out, lanes)),
            still(gains.shape),
            pl.BlockSpec(
                (1, blocks, used, lanes), lambda step: (jnp.maximum(step - chunks, 0), 0, 0, 0)
            ),
        ],
        out_shape=[
            jax.ShapeDtypeStruct(tile, jnp.bfloat16),
            jax.ShapeDtypeStruct(tile, jnp.float32),
            jax.ShapeDtypeStruct((length, total), jnp.bfloat16),
            jax.ShapeDtypeStruct((chunks, blocks, n_out, lanes), jnp.bfloat16),
            jax.ShapeDtypeStruct(gains.shape, jnp.float32),
            jax.ShapeDtypeStruct((chunks, blocks, used, lanes), jnp.bfloat16),
        ],
        scratch_shapes=[
            pltpu.VMEM(tile, jnp.float32),
            pltpu.VMEM(tile, jnp.float32),
            pltpu.VMEM(tile, jnp.bfloat16),
            pltpu.VMEM((model, length), jnp.bfloat16),
            pltpu.VMEM((chunks, length, width), jnp.float32),
            pltpu.VMEM((chunks, length, width), jnp.float32),
            pltpu.VMEM(tile, jnp.float32),
            pltpu.VMEM(tile, jnp.bfloat16),
            pltpu.VMEM((length, width), jnp.bfloat16),
            pltpu.VMEM((length, width), jnp.bfloat16),
            pltpu.VMEM((length, width), jnp.bfloat16),
            pltpu.VMEM((model, width), jnp.bfloat16),
            pltpu.VMEM((model, width), jnp.bfloat16),
            pltpu.VMEM((width, model), jnp.bfloat16),
        ],
        compiler_params=pltpu.CompilerParams(
            dimension_semantics=("arbitrary",), vmem_limit_bytes=62 * 1024 * 1024
        ),
        name="middle",
    )(heads_out, tokens, cotangent, gains, out_mat, pack)


def second_kernel(order_ref, parts_ref, out_ref, gate_ref, up_ref, down_ref):
    seqs, _, lanes = parts_ref.shape
    part_d, width = gate_ref.shape
    slabs = out_ref.shape[1] // lanes
    unit, out_rows = down_ref.shape[0] // seqs, out_ref.shape[0] // seqs
    half = lanes // 2
    n_gate, n_down = 2 * part_d, slabs * unit
    blocks = width // (seqs * unit)

    def rows_of(at, start, size):
        return parts_ref[order_ref[at], start : start + size, :].astype(jnp.float32)

    for pair in range(0, seqs, 2):
        for start, ref in ((0, gate_ref), (n_gate, up_ref)):
            for slab in range(2):
                left = rows_of(pair, start + slab * part_d, part_d)
                right = rows_of(pair + 1, start + slab * part_d, part_d)
                for side in range(2):
                    into = (2 * slab + side) * (width // blocks) + pair * unit
                    lane = slice(side * half, (side + 1) * half)
                    ref[:, into : into + lanes] = jnp.concatenate(
                        [left[:, lane], right[:, lane]], axis=1
                    )
    for at in range(seqs):
        for slab in range(slabs):
            lane = slice(slab * lanes, (slab + 1) * lanes)
            down_ref[at * unit : (at + 1) * unit, lane] = rows_of(
                at, 2 * n_gate + slab * unit, unit
            )
            out_ref[at * out_rows : (at + 1) * out_rows, lane] = rows_of(
                at, 2 * n_gate + n_down + slab * out_rows, out_rows
            )


def first_kernel(order_ref, parts_ref, query_ref, key_ref, value_ref, *, rows):
    lanes = parts_ref.shape[2]
    part_d = query_ref.shape[0]
    piece = 80
    slab = 0
    for ref in (query_ref, key_ref, value_ref):
        for local_slab in range(ref.shape[1] // lanes):
            for row in range(0, part_d, piece):
                flat = slab * part_d + row
                ref[row : row + piece, local_slab * lanes : (local_slab + 1) * lanes] = parts_ref[
                    order_ref[flat // rows], flat % rows : flat % rows + piece, :
                ].astype(jnp.float32)
            slab += 1


def unpacked(kernel, order, parts, shapes, name):
    def whole(shape):
        return pl.BlockSpec(shape, lambda step, order: (0,) * len(shape))

    return pl.pallas_call(
        kernel,
        grid_spec=pltpu.PrefetchScalarGridSpec(
            num_scalar_prefetch=1,
            grid=(1,),
            in_specs=[whole(parts.shape)],
            out_specs=[whole(shape) for shape in shapes],
        ),
        out_shape=[jax.ShapeDtypeStruct(shape, jnp.float32) for shape in shapes],
        name=name,
    )(order, parts)


def local_fast(
    tokens,
    document_ids,
    cotangent,
    w_query,
    w_key,
    w_value,
    w_out,
    w_gate,
    w_up,
    w_down,
    gain_attn_in,
    gain_attn_out,
    gain_ffn_in,
    gain_ffn_out,
    gain_query,
    gain_key,
):
    blocks = lax.axis_size("fsdp")
    place = lax.axis_index("fsdp")
    seq_at = lax.axis_index("seq")
    own_place = (seq_at % 2) * 4 + seq_at // 2
    model = w_query.shape[0] * blocks
    shard_d, shard_ff, shard_hd = w_query.shape[0], w_down.shape[0], w_out.shape[0]
    unit = shard_ff // 8
    gains = jnp.concatenate(
        [gain_attn_in, gain_attn_out, gain_ffn_in, gain_ffn_out, gain_query, gain_key]
    ).reshape(-1, LANES)
    gain_rel = gains[None]
    for bit in (1, 2):
        gain_rel = jnp.concatenate([gain_rel, permuted(gain_rel, "fsdp", bit)], axis=0)
    gain_all = jnp.stack(
        [lax.dynamic_index_in_dim(gain_rel, at ^ place, 0, keepdims=False) for at in range(blocks)]
    ).reshape(blocks, -1).astype(jnp.float32)
    norm_attn_in = gain_all[:, :shard_d].reshape(-1)
    norm_attn_out = gain_all[:, shard_d : 2 * shard_d].reshape(-1)
    norm_ffn_in = gain_all[:, 2 * shard_d : 3 * shard_d].reshape(-1)
    norm_ffn_out = gain_all[:, 3 * shard_d : 4 * shard_d].reshape(-1)
    key_part = gain_query.shape[0]
    norm_query = gain_all[:, 4 * shard_d : 4 * shard_d + key_part].reshape(-1)
    norm_key = gain_all[:, 4 * shard_d + key_part :].reshape(-1)

    first_flat = to_slabs(jnp.concatenate([w_query, w_key, w_value], axis=1))
    first_rows = first_flat.shape[0] // 8
    first_piece = lax.dynamic_slice_in_dim(first_flat, seq_at * first_rows, first_rows, 0)
    first_stages = gather_stages(first_piece, pair_gather)
    next(first_stages)
    next(first_stages)
    first_rel = next(first_stages)
    seq_order = [(at % 2) * 4 + at // 2 for at in range(8)]
    first_all = jnp.stack(
        [lax.dynamic_index_in_dim(first_rel, at ^ own_place, 0, keepdims=False) for at in seq_order],
        axis=1,
    )
    first_width = w_query.shape[1] + w_key.shape[1] + w_value.shape[1]
    qkv_mat = (
        first_all.reshape(blocks, first_width // LANES, shard_d, LANES)
        .transpose(0, 2, 1, 3)
        .reshape(model, first_width)
    )
    q_wide, k_wide = w_query.shape[1], w_key.shape[1]
    query_mat = qkv_mat[:, :q_wide]
    key_mat = qkv_mat[:, q_wide : q_wide + k_wide]
    value_mat = qkv_mat[:, q_wide + k_wide :]

    def ff_part(weight):
        weight = after(weight, first_rel)
        parts = [
            lax.dynamic_slice_in_dim(weight, block * shard_ff + seq_at * unit, unit, 1)
            for block in range(blocks)
        ]
        return jnp.concatenate(
            [jnp.concatenate(parts[at : at + 2], axis=1) for at in range(0, blocks, 2)], axis=0
        )

    gate_piece, up_piece = ff_part(w_gate), ff_part(w_up)
    down_piece = to_slabs(lax.dynamic_slice_in_dim(w_down, seq_at * unit, unit, 0))
    out_part = shard_hd // 8
    out_piece = to_slabs(lax.dynamic_slice_in_dim(w_out, seq_at * out_part, out_part, 0))
    n_gate, n_down, n_out = gate_piece.shape[0], down_piece.shape[0], out_piece.shape[0]
    second_stages = gather_stages(
        jnp.concatenate([gate_piece, up_piece, down_piece, out_piece]), line_gather
    )
    next(second_stages)
    next(second_stages)
    second_rel = next(second_stages)

    slabs_d = model // LANES
    out_rel = second_rel[:, :, 2 * n_gate + n_down :]
    out_mat = (
        jnp.stack(
            [lax.dynamic_index_in_dim(out_rel, at ^ own_place, 0, keepdims=False) for at in seq_order],
            axis=1,
        )
        .reshape(blocks, 8, slabs_d, out_part, LANES)
        .transpose(0, 1, 3, 2, 4)
        .reshape(-1, model)
    )
    inputs = tokens[0].astype(jnp.float32)
    length = inputs.shape[0]
    head_dim = key_mat.shape[1]
    heads = query_mat.shape[1] // head_dim
    offset = lax.axis_index("seq") * length
    cosine, sine_part = rope_angles(offset + jnp.arange(length, dtype=jnp.int32), head_dim)

    def query_shape(raw_rows, gain_vec):
        return rotate(
            rms_scale(raw_rows.reshape(length, heads, head_dim), gain_vec),
            cosine[:, None, :],
            sine_part[:, None, :],
        )

    def key_shape(raw_rows, gain_vec):
        return rotate(rms_scale(raw_rows, gain_vec), cosine, sine_part)

    attn_normed, pull_attn_in = jax.vjp(rms_scale, inputs, norm_attn_in)
    attn_input = attn_normed.astype(jnp.bfloat16)
    query_pre = jnp.dot(attn_input, query_mat, preferred_element_type=jnp.float32)
    key_pre = jnp.dot(attn_input, key_mat, preferred_element_type=jnp.float32)
    value_rows = jnp.dot(attn_input, value_mat, preferred_element_type=jnp.float32).astype(
        jnp.bfloat16
    )
    query_turned, pull_query = jax.vjp(query_shape, query_pre, norm_query)
    key_turned, pull_key = jax.vjp(key_shape, key_pre, norm_key)
    query_rot = query_turned.astype(jnp.bfloat16)
    key_rot = key_turned.astype(jnp.bfloat16)
    tail_rows = jnp.stack([key_rot[length - WINDOW :], value_rows[length - WINDOW :]])
    tail_prev = passed_along(tail_rows, "seq", 1)
    key_all = jnp.concatenate([tail_prev[0], key_rot], axis=0)
    value_all = jnp.concatenate([tail_prev[1], value_rows], axis=0)
    id_row = document_ids[0]
    pad_ids = jnp.concatenate([jnp.full((WINDOW,), -1, jnp.int32), id_row], axis=0)
    key_ids = lax.dynamic_slice_in_dim(pad_ids, offset, length + WINDOW, 0)
    query_ids = lax.dynamic_slice_in_dim(id_row, offset, length, 0)
    offsets = (
        jnp.arange(QBLK + WINDOW, dtype=jnp.int32)[None, :]
        - jnp.arange(QBLK, dtype=jnp.int32)[:, None]
    )
    inside = (offsets >= 1) & (offsets <= WINDOW)
    block_starts = list(range(0, length, QBLK))

    def masked_scores(block_start):
        query_block = query_rot[block_start : block_start + QBLK]
        key_block = key_all[block_start : block_start + QBLK + WINDOW]
        allowed = inside & (
            key_ids[block_start : block_start + QBLK + WINDOW][None, :]
            == query_ids[block_start : block_start + QBLK][:, None]
        )
        scores = (
            jnp.einsum("qhd,kd->hqk", query_block, key_block, preferred_element_type=jnp.float32)
            * score_scale
        )
        return jnp.where(allowed[None], scores, mask_fill)

    log_totals = []
    head_blocks = []
    for block_start in block_starts:
        masked = masked_scores(block_start)
        row_max = jnp.max(masked, axis=-1, keepdims=True)
        unnormed = jnp.exp(masked - row_max)
        row_total = jnp.sum(unnormed, axis=-1, keepdims=True)
        probs_low = (unnormed / row_total).astype(jnp.bfloat16)
        log_totals.append(row_max + jnp.log(row_total))
        head_blocks.append(
            jnp.einsum(
                "hqk,kd->qhd",
                probs_low,
                value_all[block_start : block_start + QBLK + WINDOW],
                preferred_element_type=jnp.float32,
            )
        )
    heads_out = (
        jnp.concatenate(head_blocks, axis=0).reshape(length, heads * head_dim).astype(jnp.bfloat16)
    )
    gain_rows = jnp.concatenate(
        [
            jnp.stack([norm_attn_out, norm_ffn_in, norm_ffn_out]),
            jnp.zeros((5, model), jnp.float32),
        ]
    )
    result, middle_grad, heads_low, out_abs, gain_grads, pack_grad = middle_layer(
        heads_out, tokens[0], cotangent[0], gain_rows, out_mat, second_rel, n_gate, n_down, n_out
    )
    gain_ao_grad, gain_fi_grad, gain_fo_grad = gain_grads[0], gain_grads[1], gain_grads[2]
    heads_grad = heads_low.reshape(length, heads, head_dim)
    def seq_to_rel(parts):
        rel = [j ^ own_place for j in range(8)]
        return jnp.stack(
            [
                lax.dynamic_index_in_dim(parts, (p % 4) * 2 + p // 4, 0, keepdims=False)
                for p in rel
            ]
        )

    second_parts = jnp.concatenate([pack_grad, seq_to_rel(out_abs)], axis=2)
    second_sums = reduce_stages(second_parts, line_reduce)
    key_acc = jnp.zeros((length + WINDOW, head_dim), jnp.float32)
    value_acc = jnp.zeros((length + WINDOW, head_dim), jnp.float32)
    query_grads = []
    for block_index, block_start in enumerate(block_starts):
        masked = masked_scores(block_start)
        attn_probs = jnp.exp(masked - log_totals[block_index])
        probs_low = attn_probs.astype(jnp.bfloat16)
        grad_block = heads_grad[block_start : block_start + QBLK]
        if block_index == 1:
            grad_block = after(grad_block, next(second_sums))
        query_block = query_rot[block_start : block_start + QBLK]
        key_block = key_all[block_start : block_start + QBLK + WINDOW]
        value_block = value_all[block_start : block_start + QBLK + WINDOW]
        probs_grad = jnp.einsum(
            "qhd,kd->hqk", grad_block, value_block, preferred_element_type=jnp.float32
        )
        value_acc = value_acc.at[block_start : block_start + QBLK + WINDOW].add(
            jnp.einsum("hqk,qhd->kd", probs_low, grad_block, preferred_element_type=jnp.float32)
        )
        score_grad = attn_probs * (
            probs_grad - jnp.sum(attn_probs * probs_grad, axis=-1, keepdims=True)
        )
        score_low = score_grad.astype(jnp.bfloat16)
        query_grads.append(
            jnp.einsum("hqk,kd->qhd", score_low, key_block, preferred_element_type=jnp.float32)
            * score_scale
        )
        key_acc = key_acc.at[block_start : block_start + QBLK + WINDOW].add(
            jnp.einsum("hqk,qhd->kd", score_low, query_block, preferred_element_type=jnp.float32)
            * score_scale
        )
    tail_grad = jnp.stack([key_acc[:WINDOW], value_acc[:WINDOW]])
    tail_next = passed_along(tail_grad.astype(jnp.bfloat16), "seq", -1).astype(tail_grad.dtype)
    key_own = key_acc[WINDOW:].at[length - WINDOW :].add(tail_next[0])
    value_own = value_acc[WINDOW:].at[length - WINDOW :].add(tail_next[1])
    value_low = value_own.astype(jnp.bfloat16)
    key_pre_grad, gain_k_grad = pull_key(key_own)
    query_all = after(jnp.concatenate(query_grads, axis=0), *next(second_sums))
    query_pre_grad, gain_q_grad = pull_query(query_all)
    key_low = key_pre_grad.astype(jnp.bfloat16)
    query_low = query_pre_grad.astype(jnp.bfloat16)
    query_w_grad = contract_rows(attn_input, query_low)
    key_w_grad = contract_rows(attn_input, key_low)
    value_w_grad = contract_rows(attn_input, value_low)
    attn_input_grad = (
        contract_cols(query_low, query_mat)
        + contract_cols(key_low, key_mat)
        + contract_cols(value_low, value_mat)
    )
    input_part, gain_ai_grad = pull_attn_in(attn_input_grad)
    input_grad = middle_grad + input_part
    first_grad = jnp.concatenate([query_w_grad, key_w_grad, value_w_grad], axis=1)
    first_flat_grad = (
        first_grad.astype(jnp.bfloat16)
        .reshape(blocks, shard_d, first_width // LANES, LANES)
        .transpose(0, 2, 1, 3)
        .reshape(blocks, 8, first_rows, LANES)
        .transpose(1, 0, 2, 3)
    )
    gain_parts = jnp.concatenate(
        [
            jnp.stack([gain_ai_grad, gain_ao_grad, gain_fi_grad, gain_fo_grad])
            .reshape(4, blocks, shard_d)
            .transpose(1, 0, 2)
            .reshape(blocks, -1),
            gain_q_grad.reshape(blocks, -1),
            gain_k_grad.reshape(blocks, -1),
        ],
        axis=1,
    )
    gain_width = gain_parts.shape[1] // 8
    gain_parts = gain_parts.reshape(blocks, 8, 1, gain_width).transpose(1, 0, 2, 3)
    gain_parts = jnp.pad(
        gain_parts, ((0, 0), (0, 0), (0, 15), (0, LANES - gain_width))
    ).astype(jnp.bfloat16)
    first_parts = seq_to_rel(jnp.concatenate([first_flat_grad, gain_parts], axis=2))
    first_parts = after(first_parts, next(second_sums))
    first_sums = reduce_stages(first_parts, pair_reduce)
    for _ in range(3):
        next(first_sums)
    first_final = next(first_sums)
    second_final = next(second_sums)
    order = jnp.stack([at ^ own_place for at in seq_order]).astype(jnp.int32)
    query_own, key_own_w, value_own_w = unpacked(
        lambda *refs: first_kernel(*refs, rows=first_rows),
        order,
        first_final,
        [w_query.shape, w_key.shape, w_value.shape],
        "first_own",
    )
    out_own, gate_own, up_own, down_own = unpacked(
        second_kernel,
        order,
        second_final,
        [w_out.shape, w_gate.shape, w_up.shape, w_down.shape],
        "second_own",
    )
    gain_final = jnp.stack(
        [
            lax.dynamic_slice(first_final, (order[at], first_rows, 0), (1, 1, LANES))[0, 0]
            for at in range(8)
        ]
    )
    gain_own = gain_final[:, :gain_width].reshape(-1).astype(jnp.float32)
    finals = (
        query_own,
        key_own_w,
        value_own_w,
        out_own,
        gate_own,
        up_own,
        down_own,
        gain_own[:shard_d],
        gain_own[shard_d : 2 * shard_d],
        gain_own[2 * shard_d : 3 * shard_d],
        gain_own[3 * shard_d : 4 * shard_d],
        gain_own[4 * shard_d : 4 * shard_d + key_part],
        gain_own[4 * shard_d + key_part :],
    )
    return (
        result[None],
        input_grad[None],
        finals[0],
        finals[1],
        finals[2],
        finals[3],
        finals[4],
        finals[5],
        finals[6],
        finals[7],
        finals[8],
        finals[9],
        finals[10],
        finals[11],
        finals[12],
    )


def solution(mesh):
    fits = mesh.shape["seq"] == 8 and mesh.shape["fsdp"] == 4
    placed = (
        P("fsdp", "seq", None),
        P("fsdp", None),
        P("fsdp", "seq", None),
        P("fsdp", None),
        P("fsdp", None),
        P("fsdp", None),
        P("fsdp", None),
        P("fsdp", None),
        P("fsdp", None),
        P("fsdp", None),
        P("fsdp"),
        P("fsdp"),
        P("fsdp"),
        P("fsdp"),
        P("fsdp"),
        P("fsdp"),
    )
    return jax.shard_map(
        local_fast if fits else local_generic,
        mesh=mesh,
        in_specs=placed,
        out_specs=(
            P("fsdp", "seq", None),
            P("fsdp", "seq", None),
            P("fsdp", None),
            P("fsdp", None),
            P("fsdp", None),
            P("fsdp", None),
            P("fsdp", None),
            P("fsdp", None),
            P("fsdp", None),
            P("fsdp"),
            P("fsdp"),
            P("fsdp"),
            P("fsdp"),
            P("fsdp"),
            P("fsdp"),
        ),
        check_vma=False,
    )
```

```python
import jax
import jax.numpy as jnp
from jax import lax
from jax.experimental import pallas as pl
from jax.experimental.pallas import tpu as pltpu
from jax.sharding import PartitionSpec as P

WINDOW = 512
QBLK = 512


norm_epsilon = 1e-06
rope_base = 10000.0
score_scale = 0.0625
mask_fill = -1e30


def passed_along(value, axis, steps):
    count = lax.axis_size(axis)
    initial, last = (max(0, -steps), min(count, count - steps))
    return lax.ppermute(value, axis, [(source, source + steps) for source in range(initial, last)])


def rms_scale(values, gain_vec):
    return (
        values
        * lax.rsqrt(jnp.mean(values * values, axis=-1, keepdims=True) + norm_epsilon)
        * gain_vec
    )


def rope_angles(positions, head_dim):
    freq_steps = jnp.arange(0, head_dim, 2).astype(jnp.float32) / head_dim
    inverse = jnp.exp(-jnp.log(rope_base) * freq_steps)
    angles = positions.astype(jnp.float32)[:, None] * inverse[None, :]
    return (jnp.cos(angles), jnp.sin(angles))


def rotate(values, cosine, sine_part):
    half_width = values.shape[-1] // 2
    first_half = values[..., :half_width]
    second_half = values[..., half_width:]
    return jnp.concatenate(
        [
            first_half * cosine - second_half * sine_part,
            second_half * cosine + first_half * sine_part,
        ],
        axis=-1,
    )


def gated(gate_in, up_in):
    return jax.nn.gelu(gate_in, approximate=True) * up_in


def contract_rows(left_side, right_side):
    return lax.dot_general(
        left_side, right_side, (((0,), (0,)), ((), ())), preferred_element_type=jnp.float32
    )


def contract_cols(left_side, right_side):
    return lax.dot_general(
        left_side, right_side, (((1,), (1,)), ((), ())), preferred_element_type=jnp.float32
    )


def local_generic(
    tokens,
    document_ids,
    cotangent,
    w_query,
    w_key,
    w_value,
    w_out,
    w_gate,
    w_up,
    w_down,
    gain_attn_in,
    gain_attn_out,
    gain_ffn_in,
    gain_ffn_out,
    gain_query,
    gain_key,
):
    gathered = (
        lax.all_gather(w_query, "fsdp", axis=0, tiled=True),
        lax.all_gather(w_key, "fsdp", axis=0, tiled=True),
        lax.all_gather(w_value, "fsdp", axis=0, tiled=True),
        lax.all_gather(w_out, "fsdp", axis=0, tiled=True),
        lax.all_gather(w_gate, "fsdp", axis=0, tiled=True),
        lax.all_gather(w_up, "fsdp", axis=0, tiled=True),
        lax.all_gather(w_down, "fsdp", axis=0, tiled=True),
        lax.all_gather(gain_attn_in, "fsdp", axis=0, tiled=True),
        lax.all_gather(gain_attn_out, "fsdp", axis=0, tiled=True),
        lax.all_gather(gain_ffn_in, "fsdp", axis=0, tiled=True),
        lax.all_gather(gain_ffn_out, "fsdp", axis=0, tiled=True),
        lax.all_gather(gain_query, "fsdp", axis=0, tiled=True),
        lax.all_gather(gain_key, "fsdp", axis=0, tiled=True),
    )
    query_mat, key_mat, value_mat, out_mat, gate_mat, up_mat, down_mat = (
        gathered[0],
        gathered[1],
        gathered[2],
        gathered[3],
        gathered[4],
        gathered[5],
        gathered[6],
    )
    norm_attn_in = gathered[7].astype(jnp.float32)
    norm_attn_out = gathered[8].astype(jnp.float32)
    norm_ffn_in = gathered[9].astype(jnp.float32)
    norm_ffn_out = gathered[10].astype(jnp.float32)
    norm_query = gathered[11].astype(jnp.float32)
    norm_key = gathered[12].astype(jnp.float32)
    inputs = tokens[0].astype(jnp.float32)
    length = inputs.shape[0]
    head_dim = key_mat.shape[1]
    heads = query_mat.shape[1] // head_dim
    offset = lax.axis_index("seq") * length
    cosine, sine_part = rope_angles(offset + jnp.arange(length, dtype=jnp.int32), head_dim)

    def query_shape(raw_rows, gain_vec):
        return rotate(
            rms_scale(raw_rows.reshape(length, heads, head_dim), gain_vec),
            cosine[:, None, :],
            sine_part[:, None, :],
        )

    def key_shape(raw_rows, gain_vec):
        return rotate(rms_scale(raw_rows, gain_vec), cosine, sine_part)

    attn_normed, pull_attn_in = jax.vjp(rms_scale, inputs, norm_attn_in)
    attn_input = attn_normed.astype(jnp.bfloat16)
    query_pre = jnp.dot(attn_input, query_mat, preferred_element_type=jnp.float32)
    key_pre = jnp.dot(attn_input, key_mat, preferred_element_type=jnp.float32)
    value_rows = jnp.dot(attn_input, value_mat, preferred_element_type=jnp.float32).astype(
        jnp.bfloat16
    )
    query_turned, pull_query = jax.vjp(query_shape, query_pre, norm_query)
    key_turned, pull_key = jax.vjp(key_shape, key_pre, norm_key)
    query_rot = query_turned.astype(jnp.bfloat16)
    key_rot = key_turned.astype(jnp.bfloat16)
    tail_rows = jnp.stack([key_rot[length - WINDOW + 1 :], value_rows[length - WINDOW + 1 :]])
    tail_prev = passed_along(tail_rows, "seq", 1)
    pad_row = jnp.zeros((1, head_dim), jnp.bfloat16)
    key_all = jnp.concatenate([pad_row, tail_prev[0], key_rot], axis=0)
    value_all = jnp.concatenate([pad_row, tail_prev[1], value_rows], axis=0)
    id_row = document_ids[0]
    pad_ids = jnp.concatenate([jnp.full((WINDOW,), -1, jnp.int32), id_row], axis=0)
    key_ids = lax.dynamic_slice_in_dim(pad_ids, offset, length + WINDOW, 0)
    query_ids = lax.dynamic_slice_in_dim(id_row, offset, length, 0)
    offsets = (
        jnp.arange(QBLK + WINDOW, dtype=jnp.int32)[None, :]
        - jnp.arange(QBLK, dtype=jnp.int32)[:, None]
    )
    inside = (offsets >= 1) & (offsets <= WINDOW)
    block_starts = list(range(0, length, QBLK))

    def masked_scores(block_start):
        query_block = query_rot[block_start : block_start + QBLK]
        key_block = key_all[block_start : block_start + QBLK + WINDOW]
        allowed = inside & (
            key_ids[block_start : block_start + QBLK + WINDOW][None, :]
            == query_ids[block_start : block_start + QBLK][:, None]
        )
        scores = (
            jnp.einsum("qhd,kd->hqk", query_block, key_block, preferred_element_type=jnp.float32)
            * score_scale
        )
        return jnp.where(allowed[None], scores, mask_fill)

    log_totals = []
    head_blocks = []
    for block_start in block_starts:
        masked = masked_scores(block_start)
        row_max = jnp.max(masked, axis=-1, keepdims=True)
        unnormed = jnp.exp(masked - row_max)
        row_total = jnp.sum(unnormed, axis=-1, keepdims=True)
        probs_low = (unnormed / row_total).astype(jnp.bfloat16)
        log_totals.append(row_max + jnp.log(row_total))
        head_blocks.append(
            jnp.einsum(
                "hqk,kd->qhd",
                probs_low,
                value_all[block_start : block_start + QBLK + WINDOW],
                preferred_element_type=jnp.float32,
            )
        )
    heads_out = (
        jnp.concatenate(head_blocks, axis=0).reshape(length, heads * head_dim).astype(jnp.bfloat16)
    )
    attn_proj = jnp.dot(heads_out, out_mat, preferred_element_type=jnp.float32)
    attn_normed_out, pull_attn_out = jax.vjp(rms_scale, attn_proj, norm_attn_out)
    middle = inputs + attn_normed_out
    ffn_normed, pull_ffn_in = jax.vjp(rms_scale, middle, norm_ffn_in)
    ffn_input = ffn_normed.astype(jnp.bfloat16)
    gate_pre = jnp.dot(ffn_input, gate_mat, preferred_element_type=jnp.float32)
    up_pre = jnp.dot(ffn_input, up_mat, preferred_element_type=jnp.float32)
    hidden_full, pull_gelu = jax.vjp(gated, gate_pre, up_pre)
    hidden = hidden_full.astype(jnp.bfloat16)
    ffn_out = jnp.dot(hidden, down_mat, preferred_element_type=jnp.float32)
    ffn_normed_out, pull_ffn_out = jax.vjp(rms_scale, ffn_out, norm_ffn_out)
    result = middle + ffn_normed_out
    out_grad = cotangent[0].astype(jnp.float32)
    ffn_out_grad, gain_fo_grad = pull_ffn_out(out_grad)
    ffn_out_low = ffn_out_grad.astype(jnp.bfloat16)
    down_w_grad = contract_rows(hidden, ffn_out_low)
    hidden_grad = contract_cols(ffn_out_low, down_mat)
    gate_grad, up_grad = pull_gelu(hidden_grad)
    gate_low = gate_grad.astype(jnp.bfloat16)
    up_low = up_grad.astype(jnp.bfloat16)
    gate_w_grad = contract_rows(ffn_input, gate_low)
    up_w_grad = contract_rows(ffn_input, up_low)
    ffn_input_grad = contract_cols(gate_low, gate_mat) + contract_cols(up_low, up_mat)
    middle_part, gain_fi_grad = pull_ffn_in(ffn_input_grad)
    middle_grad = out_grad + middle_part
    attn_proj_grad, gain_ao_grad = pull_attn_out(middle_grad)
    proj_low = attn_proj_grad.astype(jnp.bfloat16)
    out_w_grad = contract_rows(heads_out, proj_low)
    heads_grad = (
        contract_cols(proj_low, out_mat).astype(jnp.bfloat16).reshape(length, heads, head_dim)
    )
    key_acc = jnp.zeros((length + WINDOW, head_dim), jnp.float32)
    value_acc = jnp.zeros((length + WINDOW, head_dim), jnp.float32)
    query_grads = []
    for block_index, block_start in enumerate(block_starts):
        masked = masked_scores(block_start)
        attn_probs = jnp.exp(masked - log_totals[block_index])
        probs_low = attn_probs.astype(jnp.bfloat16)
        grad_block = heads_grad[block_start : block_start + QBLK]
        query_block = query_rot[block_start : block_start + QBLK]
        key_block = key_all[block_start : block_start + QBLK + WINDOW]
        value_block = value_all[block_start : block_start + QBLK + WINDOW]
        probs_grad = jnp.einsum(
            "qhd,kd->hqk", grad_block, value_block, preferred_element_type=jnp.float32
        )
        value_acc = value_acc.at[block_start : block_start + QBLK + WINDOW].add(
            jnp.einsum("hqk,qhd->kd", probs_low, grad_block, preferred_element_type=jnp.float32)
        )
        score_grad = attn_probs * (
            probs_grad - jnp.sum(attn_probs * probs_grad, axis=-1, keepdims=True)
        )
        score_low = score_grad.astype(jnp.bfloat16)
        query_grads.append(
            jnp.einsum("hqk,kd->qhd", score_low, key_block, preferred_element_type=jnp.float32)
            * score_scale
        )
        key_acc = key_acc.at[block_start : block_start + QBLK + WINDOW].add(
            jnp.einsum("hqk,qhd->kd", score_low, query_block, preferred_element_type=jnp.float32)
            * score_scale
        )
    tail_grad = jnp.stack([key_acc[1:WINDOW], value_acc[1:WINDOW]])
    tail_next = passed_along(tail_grad.astype(jnp.bfloat16), "seq", -1).astype(tail_grad.dtype)
    key_own = key_acc[WINDOW:].at[length - WINDOW + 1 :].add(tail_next[0])
    value_own = value_acc[WINDOW:].at[length - WINDOW + 1 :].add(tail_next[1])
    value_low = value_own.astype(jnp.bfloat16)
    key_pre_grad, gain_k_grad = pull_key(key_own)
    query_pre_grad, gain_q_grad = pull_query(jnp.concatenate(query_grads, axis=0))
    key_low = key_pre_grad.astype(jnp.bfloat16)
    query_low = query_pre_grad.astype(jnp.bfloat16)
    query_w_grad = contract_rows(attn_input, query_low)
    key_w_grad = contract_rows(attn_input, key_low)
    value_w_grad = contract_rows(attn_input, value_low)
    attn_input_grad = (
        contract_cols(query_low, query_mat)
        + contract_cols(key_low, key_mat)
        + contract_cols(value_low, value_mat)
    )
    input_part, gain_ai_grad = pull_attn_in(attn_input_grad)
    input_grad = middle_grad + input_part
    row_parts = (
        lax.psum_scatter(query_w_grad, "fsdp", scatter_dimension=0, tiled=True),
        lax.psum_scatter(key_w_grad, "fsdp", scatter_dimension=0, tiled=True),
        lax.psum_scatter(value_w_grad, "fsdp", scatter_dimension=0, tiled=True),
        lax.psum_scatter(out_w_grad, "fsdp", scatter_dimension=0, tiled=True),
        lax.psum_scatter(gate_w_grad, "fsdp", scatter_dimension=0, tiled=True),
        lax.psum_scatter(up_w_grad, "fsdp", scatter_dimension=0, tiled=True),
        lax.psum_scatter(down_w_grad, "fsdp", scatter_dimension=0, tiled=True),
        lax.psum_scatter(gain_ai_grad, "fsdp", scatter_dimension=0, tiled=True),
        lax.psum_scatter(gain_ao_grad, "fsdp", scatter_dimension=0, tiled=True),
        lax.psum_scatter(gain_fi_grad, "fsdp", scatter_dimension=0, tiled=True),
        lax.psum_scatter(gain_fo_grad, "fsdp", scatter_dimension=0, tiled=True),
        lax.psum_scatter(gain_q_grad, "fsdp", scatter_dimension=0, tiled=True),
        lax.psum_scatter(gain_k_grad, "fsdp", scatter_dimension=0, tiled=True),
    )
    finals = lax.psum(
        (
            row_parts[0],
            row_parts[1],
            row_parts[2],
            row_parts[3],
            row_parts[4],
            row_parts[5],
            row_parts[6],
            row_parts[7],
            row_parts[8],
            row_parts[9],
            row_parts[10],
            row_parts[11],
            row_parts[12],
        ),
        "seq",
    )
    return (
        result.astype(jnp.bfloat16)[None],
        input_grad[None],
        finals[0],
        finals[1],
        finals[2],
        finals[3],
        finals[4],
        finals[5],
        finals[6],
        finals[7],
        finals[8],
        finals[9],
        finals[10],
        finals[11],
        finals[12],
    )


LANES = 128


def permuted(value, axis, bit):
    count = lax.axis_size(axis)
    return lax.ppermute(value, axis, [(at, at ^ bit) for at in range(count)])


def added(left, right):
    return left.astype(jnp.float32) + right.astype(jnp.float32)


def half_rows(rows):
    return (rows // 2 + 15) // 16 * 16


def chips_gather(first, second):
    ones, twos = [first], [second]
    for bit in (2, 4):
        ones = ones + [permuted(item, "seq", bit) for item in ones]
    for bit in (4, 2):
        twos = twos + [permuted(item, "seq", bit) for item in twos]
    return [
        jnp.concatenate([ones[x + 2 * y], twos[y + 2 * x]], axis=0) for y in (0, 1) for x in (0, 1)
    ]


def line_gather(piece):
    count = lax.axis_size("fsdp")
    place = lax.axis_index("fsdp")
    zeros = (0,) * piece.ndim
    table = jnp.zeros((3 * count - 2,) + piece.shape, piece.dtype)
    table = lax.dynamic_update_slice(table, piece[None], (place + count - 1,) + zeros)
    right, left = piece, piece
    for step in range(1, count):
        right = lax.ppermute(right, "fsdp", [(at, at + 1) for at in range(step - 1, count - 1)])
        left = lax.ppermute(left, "fsdp", [(at, at - 1) for at in range(1, count - step + 1)])
        table = lax.dynamic_update_slice(table, right[None], (place - step + count - 1,) + zeros)
        table = lax.dynamic_update_slice(table, left[None], (place + step + count - 1,) + zeros)
    return table[count - 1 : 2 * count - 1]


def after(value, *others):
    return lax.optimization_barrier((value,) + others)[0]


def pair_gather(piece):
    count = lax.axis_size("fsdp")
    place = lax.axis_index("fsdp")
    rel, bit = piece[None], 1
    while bit < count:
        rel = jnp.concatenate([rel, permuted(rel, "fsdp", bit)], axis=0)
        bit *= 2
    return jnp.stack(
        [lax.dynamic_index_in_dim(rel, at ^ place, 0, keepdims=False) for at in range(count)]
    )


def pair_reduce(own):
    place = lax.axis_index("fsdp")
    bit = lax.axis_size("fsdp") // 2
    while bit:
        mine = (place // bit) % 2
        halves = own.reshape((2, bit) + own.shape[1:])
        sent = lax.dynamic_index_in_dim(halves, 1 - mine, 0, keepdims=False)
        kept = lax.dynamic_index_in_dim(halves, mine, 0, keepdims=False)
        total = added(kept, permuted(sent, "fsdp", bit))
        own = total.astype(jnp.bfloat16)
        bit //= 2
    return total[0]


def line_reduce(own):
    count = lax.axis_size("fsdp")
    place = lax.axis_index("fsdp")

    def at(index):
        return lax.dynamic_index_in_dim(own, index, 0, keepdims=False)

    right, left = None, None
    for step in range(count - 1):
        up = at(jnp.minimum(count - 1 - step + place, count - 1))
        down = at(jnp.maximum(step - (count - 1) + place, 0))
        if right is not None:
            up = added(up, right).astype(jnp.bfloat16)
            down = added(down, left).astype(jnp.bfloat16)
        right = lax.ppermute(up, "fsdp", [(at_, at_ + 1) for at_ in range(min(step, count - 2) + 1)])
        left = lax.ppermute(
            down, "fsdp", [(at_, at_ - 1) for at_ in range(max(count - 1 - step, 1), count)]
        )
    return added(at(place), right) + left.astype(jnp.float32)


def gather_stages(piece, along):
    whole = along(piece)
    yield whole
    half = whole.shape[0] // 2
    first, second = whole[:half], whole[half:]
    own = jnp.stack(chips_gather(first, second))
    yield own
    yield jnp.concatenate([own, permuted(own, "seq", 1)], axis=0)


def reduce_stages(parts, along):
    half = parts.shape[1] // 2
    mine = added(parts[:4], permuted(parts[4:], "seq", 1)).astype(jnp.bfloat16)
    yield mine
    ones, twos = mine[:, :half], mine[:, half:]
    ones = added(ones[0::2], permuted(ones[1::2], "seq", 2)).astype(jnp.bfloat16)
    twos = added(twos[:2], permuted(twos[2:], "seq", 4)).astype(jnp.bfloat16)
    yield (ones, twos)
    ones = added(ones[0], permuted(ones[1], "seq", 4)).astype(jnp.bfloat16)
    twos = added(twos[0], permuted(twos[1], "seq", 2)).astype(jnp.bfloat16)
    own = jnp.concatenate([ones, twos], axis=0)
    yield own
    low = along(own).astype(jnp.bfloat16)
    cut = half_rows(low.shape[0])
    ours = jnp.stack(chips_gather(low[:cut], low[cut:]))
    yield jnp.concatenate([ours, permuted(ours, "seq", 1)], axis=0)


def to_slabs(rows):
    height, width = rows.shape
    return rows.reshape(height, width // LANES, LANES).transpose(1, 0, 2).reshape(-1, LANES)


def from_slabs(rows, width):
    count = width // LANES
    return rows.reshape(count, -1, LANES).transpose(1, 0, 2).reshape(-1, width)


def totals_of(vector):
    for axis in ("seq", "fsdp"):
        bit = 1
        while bit < lax.axis_size(axis):
            vector = vector + permuted(vector, axis, bit)
            bit *= 2
    return vector

TOK_BLK = 256
gelu_scale = 0.7978845608028654
gelu_cubic = 0.044715


def dot_cols(left_side, right_side):
    return lax.dot_general(
        left_side, right_side, (((1,), (1,)), ((), ())), preferred_element_type=jnp.float32
    )


def dot_plain(left_side, right_side):
    return jnp.dot(left_side, right_side, preferred_element_type=jnp.float32)


def row_rate(rows):
    return lax.rsqrt(jnp.mean(rows * rows, axis=-1, keepdims=True) + norm_epsilon)


def norm_back(rows, gain_row, grad):
    rate = row_rate(rows)
    scaled = gain_row * grad
    back = rate * scaled - rows * (
        rate * rate * rate * jnp.mean(rows * scaled, axis=-1, keepdims=True)
    )
    return back, jnp.sum(rows * rate * grad, axis=0, keepdims=True)


def middle_kernel(
    heads_ref,
    tok_ref,
    cot_ref,
    gain_ref,
    out_w_ref,
    pack_ref,
    result_ref,
    mid_grad_ref,
    heads_grad_ref,
    out_grad_ref,
    gain_grad_ref,
    pack_grad_ref,
    proj_sc,
    mid_sc,
    norm_sc,
    turn_sc,
    gate_sc,
    up_sc,
    acc_sc,
    back_sc,
    gate_low_sc,
    up_low_sc,
    hid_low_sc,
    gate_w_sc,
    up_w_sc,
    down_w_sc,
):
    step = pl.program_id(0)
    blocks, _, lanes = pack_ref.shape[1:]
    length, model = tok_ref.shape
    part_d = model // blocks
    wide = gate_w_sc.shape[1] // lanes
    slabs = model // lanes
    unit = gate_w_sc.shape[1] // blocks
    rows_g = wide * part_d
    chunks = gate_sc.shape[0]
    chunk = lax.rem(step, chunks)

    for block in range(blocks):
        for slab in range(wide):
            take = slice(slab * part_d, (slab + 1) * part_d)
            also = slice(rows_g + slab * part_d, rows_g + (slab + 1) * part_d)
            into = slice(block * part_d, (block + 1) * part_d)
            lane = slice(slab * lanes, (slab + 1) * lanes)
            gate_w_sc[into, lane] = pack_ref[0, block, take, :]
            up_w_sc[into, lane] = pack_ref[0, block, also, :]
        for slab in range(slabs):
            take = slice(2 * rows_g + slab * unit, 2 * rows_g + (slab + 1) * unit)
            down_w_sc[block * unit : (block + 1) * unit, slab * lanes : (slab + 1) * lanes] = (
                pack_ref[0, block, take, :]
            )

    gain_ao, gain_fi, gain_fo = gain_ref[0:1], gain_ref[1:2], gain_ref[2:3]

    def each(body):
        def wrapped(at, carry):
            body(pl.ds(pl.multiple_of(at * TOK_BLK, TOK_BLK), TOK_BLK))
            return carry

        lax.fori_loop(0, length // TOK_BLK, wrapped, 0)

    @pl.when(step == 0)
    def _():
        gain_grad_ref[...] = jnp.zeros_like(gain_grad_ref)

        def start(rows):
            proj = dot_plain(heads_ref[rows, :], out_w_ref[...])
            proj_sc[rows, :] = proj
            middle = tok_ref[rows, :].astype(jnp.float32) + proj * row_rate(proj) * gain_ao
            mid_sc[rows, :] = middle
            norm_sc[rows, :] = (middle * row_rate(middle) * gain_fi).astype(jnp.bfloat16)
            acc_sc[rows, :] = jnp.zeros((TOK_BLK, model), jnp.float32)

        each(start)
        for at in range(length // TOK_BLK):
            rows = slice(at * TOK_BLK, (at + 1) * TOK_BLK)
            turn_sc[:, rows] = norm_sc[rows, :].T

    @pl.when(step < chunks)
    def _():
        def forward(rows):
            gate = dot_plain(norm_sc[rows, :], gate_w_sc[...])
            up = dot_plain(norm_sc[rows, :], up_w_sc[...])
            gate_sc[chunk, rows, :] = gate
            up_sc[chunk, rows, :] = up
            inner = jnp.tanh(gelu_scale * (gate + gelu_cubic * (gate * gate * gate)))
            hidden = (0.5 * gate * (1.0 + inner) * up).astype(jnp.bfloat16)
            acc_sc[rows, :] += dot_plain(hidden, down_w_sc[...])

        each(forward)

    @pl.when(step == chunks)
    def _():
        def turn(rows):
            ffn = acc_sc[rows, :]
            result_ref[rows, :] = (mid_sc[rows, :] + ffn * row_rate(ffn) * gain_fo).astype(
                jnp.bfloat16
            )
            back, gain_part = norm_back(ffn, gain_fo, cot_ref[rows, :].astype(jnp.float32))
            back_sc[rows, :] = back.astype(jnp.bfloat16)
            gain_grad_ref[2:3, :] += gain_part
            acc_sc[rows, :] = jnp.zeros((TOK_BLK, model), jnp.float32)

        each(turn)

    @pl.when(step >= chunks)
    def _():
        def backward(rows):
            gate = gate_sc[chunk, rows, :]
            up = up_sc[chunk, rows, :]
            square = gate * gate
            inner = jnp.tanh(gelu_scale * (gate + gelu_cubic * (square * gate)))
            half = 0.5 * (1.0 + inner)
            active = gate * half
            slope = half + (0.5 * gelu_scale) * gate * (1.0 - inner * inner) * (
                1.0 + 3.0 * gelu_cubic * square
            )
            hid_grad = dot_cols(back_sc[rows, :], down_w_sc[...])
            gate_low = (hid_grad * up * slope).astype(jnp.bfloat16)
            up_low = (hid_grad * active).astype(jnp.bfloat16)
            gate_low_sc[rows, :] = gate_low
            up_low_sc[rows, :] = up_low
            hid_low_sc[rows, :] = (active * up).astype(jnp.bfloat16)
            acc_sc[rows, :] += dot_cols(gate_low, gate_w_sc[...]) + dot_cols(
                up_low, up_w_sc[...]
            )

        each(backward)
        gate_grad = dot_plain(turn_sc[...], gate_low_sc[...]).astype(jnp.bfloat16)
        up_grad = dot_plain(turn_sc[...], up_low_sc[...]).astype(jnp.bfloat16)
        for block in range(blocks):
            for slab in range(wide):
                take = slice(slab * part_d, (slab + 1) * part_d)
                also = slice(rows_g + slab * part_d, rows_g + (slab + 1) * part_d)
                into = slice(block * part_d, (block + 1) * part_d)
                lane = slice(slab * lanes, (slab + 1) * lanes)
                pack_grad_ref[0, block, take, :] = gate_grad[into, lane]
                pack_grad_ref[0, block, also, :] = up_grad[into, lane]
        down_grad = lax.dot_general(
            hid_low_sc[...], back_sc[...], (((0,), (0,)), ((), ())),
            preferred_element_type=jnp.float32,
        ).astype(jnp.bfloat16)
        for block in range(blocks):
            for slab in range(slabs):
                take = slice(2 * rows_g + slab * unit, 2 * rows_g + (slab + 1) * unit)
                pack_grad_ref[0, block, take, :] = down_grad[
                    block * unit : (block + 1) * unit, slab * lanes : (slab + 1) * lanes
                ]

    @pl.when(step == 2 * chunks - 1)
    def _():
        def finish(rows):
            middle = mid_sc[rows, :]
            part, gain_part = norm_back(middle, gain_fi, acc_sc[rows, :])
            gain_grad_ref[1:2, :] += gain_part
            mid_grad = cot_ref[rows, :].astype(jnp.float32) + part
            mid_grad_ref[rows, :] = mid_grad
            proj_grad, gain_part = norm_back(proj_sc[rows, :], gain_ao, mid_grad)
            gain_grad_ref[0:1, :] += gain_part
            low = proj_grad.astype(jnp.bfloat16)
            norm_sc[rows, :] = low
            heads_grad_ref[rows, :] = dot_cols(low, out_w_ref[...]).astype(jnp.bfloat16)

        each(finish)
        share = heads_ref.shape[1] // blocks
        out_rows = out_grad_ref.shape[2] // slabs
        for block in range(blocks):
            grad = lax.dot_general(
                heads_ref[:, block * share : (block + 1) * share], norm_sc[...],
                (((0,), (0,)), ((), ())),
                preferred_element_type=jnp.float32,
            ).astype(jnp.bfloat16)
            for at in range(out_grad_ref.shape[0]):
                for slab in range(slabs):
                    out_grad_ref[at, block, slab * out_rows : (slab + 1) * out_rows, :] = grad[
                        at * out_rows : (at + 1) * out_rows, slab * lanes : (slab + 1) * lanes
                    ]


def middle_layer(heads_out, tokens, cotangent, gains, out_mat, pack, n_gate, n_down, n_out):
    length, model = tokens.shape
    chunks, blocks, rows, lanes = pack.shape
    used = 2 * n_gate + n_down
    width = n_gate * blocks * lanes // model
    total = heads_out.shape[1]

    def still(shape):
        return pl.BlockSpec(
            shape, lambda step: (0,) * len(shape), pipeline_mode=pl.Buffered(1)
        )

    tile = (length, model)
    return pl.pallas_call(
        middle_kernel,
        grid=(2 * chunks,),
        in_specs=[
            still((length, total)),
            still(tile),
            still(tile),
            still(gains.shape),
            still(out_mat.shape),
            pl.BlockSpec((1, blocks, rows, lanes), lambda step: (lax.rem(step, chunks), 0, 0, 0)),
        ],
        out_specs=[
            still(tile),
            still(tile),
            still((length, total)),
            still((chunks, blocks, n_out, lanes)),
            still(gains.shape),
            pl.BlockSpec(
                (1, blocks, used, lanes), lambda step: (jnp.maximum(step - chunks, 0), 0, 0, 0)
            ),
        ],
        out_shape=[
            jax.ShapeDtypeStruct(tile, jnp.bfloat16),
            jax.ShapeDtypeStruct(tile, jnp.float32),
            jax.ShapeDtypeStruct((length, total), jnp.bfloat16),
            jax.ShapeDtypeStruct((chunks, blocks, n_out, lanes), jnp.bfloat16),
            jax.ShapeDtypeStruct(gains.shape, jnp.float32),
            jax.ShapeDtypeStruct((chunks, blocks, used, lanes), jnp.bfloat16),
        ],
        scratch_shapes=[
            pltpu.VMEM(tile, jnp.float32),
            pltpu.VMEM(tile, jnp.float32),
            pltpu.VMEM(tile, jnp.bfloat16),
            pltpu.VMEM((model, length), jnp.bfloat16),
            pltpu.VMEM((chunks, length, width), jnp.float32),
            pltpu.VMEM((chunks, length, width), jnp.float32),
            pltpu.VMEM(tile, jnp.float32),
            pltpu.VMEM(tile, jnp.bfloat16),
            pltpu.VMEM((length, width), jnp.bfloat16),
            pltpu.VMEM((length, width), jnp.bfloat16),
            pltpu.VMEM((length, width), jnp.bfloat16),
            pltpu.VMEM((model, width), jnp.bfloat16),
            pltpu.VMEM((model, width), jnp.bfloat16),
            pltpu.VMEM((width, model), jnp.bfloat16),
        ],
        compiler_params=pltpu.CompilerParams(
            dimension_semantics=("arbitrary",), vmem_limit_bytes=62 * 1024 * 1024
        ),
        name="middle",
    )(heads_out, tokens, cotangent, gains, out_mat, pack)


def second_kernel(order_ref, parts_ref, out_ref, gate_ref, up_ref, down_ref):
    seqs, _, lanes = parts_ref.shape
    part_d, width = gate_ref.shape
    slabs = out_ref.shape[1] // lanes
    unit, out_rows = down_ref.shape[0] // seqs, out_ref.shape[0] // seqs
    half = lanes // 2
    n_gate, n_down = 2 * part_d, slabs * unit
    blocks = width // (seqs * unit)

    def rows_of(at, start, size):
        return parts_ref[order_ref[at], start : start + size, :].astype(jnp.float32)

    for pair in range(0, seqs, 2):
        for start, ref in ((0, gate_ref), (n_gate, up_ref)):
            for slab in range(2):
                left = rows_of(pair, start + slab * part_d, part_d)
                right = rows_of(pair + 1, start + slab * part_d, part_d)
                for side in range(2):
                    into = (2 * slab + side) * (width // blocks) + pair * unit
                    lane = slice(side * half, (side + 1) * half)
                    ref[:, into : into + lanes] = jnp.concatenate(
                        [left[:, lane], right[:, lane]], axis=1
                    )
    for at in range(seqs):
        for slab in range(slabs):
            lane = slice(slab * lanes, (slab + 1) * lanes)
            down_ref[at * unit : (at + 1) * unit, lane] = rows_of(
                at, 2 * n_gate + slab * unit, unit
            )
            out_ref[at * out_rows : (at + 1) * out_rows, lane] = rows_of(
                at, 2 * n_gate + n_down + slab * out_rows, out_rows
            )


def first_kernel(order_ref, parts_ref, query_ref, key_ref, value_ref, *, rows):
    lanes = parts_ref.shape[2]
    part_d = query_ref.shape[0]
    piece = 80
    slab = 0
    for ref in (query_ref, key_ref, value_ref):
        for local_slab in range(ref.shape[1] // lanes):
            for row in range(0, part_d, piece):
                flat = slab * part_d + row
                ref[row : row + piece, local_slab * lanes : (local_slab + 1) * lanes] = parts_ref[
                    order_ref[flat // rows], flat % rows : flat % rows + piece, :
                ].astype(jnp.float32)
            slab += 1


def unpacked(kernel, order, parts, shapes, name):
    def whole(shape):
        return pl.BlockSpec(shape, lambda step, order: (0,) * len(shape))

    return pl.pallas_call(
        kernel,
        grid_spec=pltpu.PrefetchScalarGridSpec(
            num_scalar_prefetch=1,
            grid=(1,),
            in_specs=[whole(parts.shape)],
            out_specs=[whole(shape) for shape in shapes],
        ),
        out_shape=[jax.ShapeDtypeStruct(shape, jnp.float32) for shape in shapes],
        name=name,
    )(order, parts)


ATT_TILE = 256


def attention_back_kernel(
    q_ref, grad_ref, key_ref, value_ref, qid_ref, kid_ref, dq_ref, dk_ref, dv_ref, *, start
):
    @pl.when(pl.program_id(0) == 0)
    def _():
        dk_ref[...] = jnp.zeros_like(dk_ref)
        dv_ref[...] = jnp.zeros_like(dv_ref)

    span = ATT_TILE + WINDOW
    shape = (ATT_TILE, span)
    offsets = lax.broadcasted_iota(jnp.int32, shape, 1) - lax.broadcasted_iota(
        jnp.int32, shape, 0
    )
    inside = (offsets >= 1) & (offsets <= WINDOW)
    for first in range(0, q_ref.shape[0], ATT_TILE):
        rows = slice(first, first + ATT_TILE)
        keys = slice(start + first, start + first + span)
        into = slice(first, first + span)
        query, grad = q_ref[rows, :], grad_ref[rows, :]
        key, value = key_ref[keys, :], value_ref[keys, :]
        allowed = inside & (kid_ref[:, keys] == qid_ref[rows, :])
        masked = jnp.where(allowed, dot_cols(query, key) * score_scale, mask_fill)
        unnormed = jnp.exp(masked - jnp.max(masked, axis=-1, keepdims=True))
        probs = unnormed * (1.0 / jnp.sum(unnormed, axis=-1, keepdims=True))
        probs_grad = dot_cols(grad, value)
        score_grad = probs * (probs_grad - jnp.sum(probs * probs_grad, axis=-1, keepdims=True))
        score_low = score_grad.astype(jnp.bfloat16)
        dv_ref[into, :] += contract_rows(probs.astype(jnp.bfloat16), grad)
        dk_ref[into, :] += contract_rows(score_low, query) * score_scale
        dq_ref[rows, :] = dot_plain(score_low, key) * score_scale


def attention_back(query_flat, grad_flat, key_all, value_all, query_ids, key_ids, block):
    length, total = query_flat.shape
    head_dim = key_all.shape[1]
    window = QBLK + WINDOW

    def whole(shape):
        return pl.BlockSpec(shape, lambda head: (0,) * len(shape))

    side = pl.BlockSpec((QBLK, head_dim), lambda head: (block, head))
    return pl.pallas_call(
        lambda *refs: attention_back_kernel(*refs, start=block * QBLK),
        grid=(total // head_dim,),
        in_specs=[
            side,
            side,
            whole(key_all.shape),
            whole(value_all.shape),
            pl.BlockSpec((QBLK, 1), lambda head: (block, 0)),
            whole((1, length + WINDOW)),
        ],
        out_specs=[
            pl.BlockSpec((QBLK, head_dim), lambda head: (0, head)),
            whole((window, head_dim)),
            whole((window, head_dim)),
        ],
        out_shape=[
            jax.ShapeDtypeStruct((QBLK, total), jnp.float32),
            jax.ShapeDtypeStruct((window, head_dim), jnp.float32),
            jax.ShapeDtypeStruct((window, head_dim), jnp.float32),
        ],
        compiler_params=pltpu.CompilerParams(
            dimension_semantics=("arbitrary",), vmem_limit_bytes=48 * 1024 * 1024
        ),
        name="attention_back",
    )(query_flat, grad_flat, key_all, value_all, query_ids[:, None], key_ids[None, :])


def projection_back_kernel(
    tok_ref,
    mid_grad_ref,
    dq_ref,
    dk_ref,
    dv_ref,
    cos_ref,
    sin_ref,
    gain_ref,
    gain_head_ref,
    mat_ref,
    input_grad_ref,
    weight_ref,
    gain_grad_ref,
    gain_head_grad_ref,
    acc_sc,
    low_sc,
    *,
    rows,
):
    step = pl.program_id(0)
    lanes = weight_ref.shape[3]
    head_dim = dk_ref.shape[1]
    half = head_dim // 2
    total = dq_ref.shape[1]

    @pl.when(step == 0)
    def _():
        acc_sc[...] = jnp.zeros_like(acc_sc)
        gain_grad_ref[...] = jnp.zeros_like(gain_grad_ref)
        gain_head_grad_ref[...] = jnp.zeros_like(gain_head_grad_ref)

    inputs = tok_ref[...].astype(jnp.float32)
    normed = (inputs * row_rate(inputs) * gain_ref[0:1]).astype(jnp.bfloat16)
    cosine, sine_part = cos_ref[...], sin_ref[...]

    def turned_back(grad):
        one, two = grad[:, :half], grad[:, half:]
        return jnp.concatenate(
            [one * cosine + two * sine_part, two * cosine - one * sine_part], axis=1
        )

    gain_q, gain_k = gain_head_ref[0:1], gain_head_ref[1:2]
    for first in range(0, total, head_dim):
        lane = slice(first, first + head_dim)
        pre = dot_plain(normed, mat_ref[:, lane])
        back, gain_part = norm_back(pre, gain_q, turned_back(dq_ref[:, lane]))
        gain_head_grad_ref[0:1, :] += gain_part
        low_sc[:, lane] = back.astype(jnp.bfloat16)
    lane = slice(total, total + head_dim)
    pre = dot_plain(normed, mat_ref[:, lane])
    back, gain_part = norm_back(pre, gain_k, turned_back(dk_ref[...]))
    gain_head_grad_ref[1:2, :] += gain_part
    low_sc[:, lane] = back.astype(jnp.bfloat16)
    low_sc[:, total + head_dim :] = dv_ref[...].astype(jnp.bfloat16)

    acc_sc[...] += contract_rows(normed, low_sc[...])
    part, gain_part = norm_back(inputs, gain_ref[0:1], dot_cols(low_sc[...], mat_ref[...]))
    input_grad_ref[...] = mid_grad_ref[...] + part
    gain_grad_ref[0:1, :] += gain_part

    @pl.when(step == pl.num_programs(0) - 1)
    def _():
        blocks = weight_ref.shape[1]
        part_d = acc_sc.shape[0] // blocks
        piece = 80
        for block in range(blocks):
            for slab in range(acc_sc.shape[1] // lanes):
                for row in range(0, part_d, piece):
                    flat = slab * part_d + row
                    weight_ref[flat // rows, block, flat % rows : flat % rows + piece, :] = acc_sc[
                        block * part_d + row : block * part_d + row + piece,
                        slab * lanes : (slab + 1) * lanes,
                    ].astype(jnp.bfloat16)


def projection_back(
    tokens, middle_grad, dq, dk, dv, cosine, sine_part, gain, gain_heads, qkv_mat, blocks, rows
):
    length, model = tokens.shape
    tile = 256

    def whole(shape):
        return pl.BlockSpec(shape, lambda step: (0,) * len(shape))

    def part(width):
        return pl.BlockSpec((tile, width), lambda step: (step, 0))

    packed = (8, blocks, rows, LANES)
    return pl.pallas_call(
        lambda *refs: projection_back_kernel(*refs, rows=rows),
        grid=(length // tile,),
        in_specs=[
            part(model),
            part(model),
            part(dq.shape[1]),
            part(dk.shape[1]),
            part(dv.shape[1]),
            part(cosine.shape[1]),
            part(cosine.shape[1]),
            whole(gain.shape),
            whole(gain_heads.shape),
            whole(qkv_mat.shape),
        ],
        out_specs=[part(model), whole(packed), whole(gain.shape), whole(gain_heads.shape)],
        out_shape=[
            jax.ShapeDtypeStruct((length, model), jnp.float32),
            jax.ShapeDtypeStruct(packed, jnp.bfloat16),
            jax.ShapeDtypeStruct(gain.shape, jnp.float32),
            jax.ShapeDtypeStruct(gain_heads.shape, jnp.float32),
        ],
        scratch_shapes=[
            pltpu.VMEM((model, qkv_mat.shape[1]), jnp.float32),
            pltpu.VMEM((tile, qkv_mat.shape[1]), jnp.bfloat16),
        ],
        compiler_params=pltpu.CompilerParams(
            dimension_semantics=("arbitrary",), vmem_limit_bytes=48 * 1024 * 1024
        ),
        name="projection_back",
    )(tokens, middle_grad, dq, dk, dv, cosine, sine_part, gain, gain_heads, qkv_mat)


def local_fast(
    tokens,
    document_ids,
    cotangent,
    w_query,
    w_key,
    w_value,
    w_out,
    w_gate,
    w_up,
    w_down,
    gain_attn_in,
    gain_attn_out,
    gain_ffn_in,
    gain_ffn_out,
    gain_query,
    gain_key,
):
    blocks = lax.axis_size("fsdp")
    place = lax.axis_index("fsdp")
    seq_at = lax.axis_index("seq")
    own_place = (seq_at % 2) * 4 + seq_at // 2
    model = w_query.shape[0] * blocks
    shard_d, shard_ff, shard_hd = w_query.shape[0], w_down.shape[0], w_out.shape[0]
    unit = shard_ff // 8
    gains = jnp.concatenate(
        [gain_attn_in, gain_attn_out, gain_ffn_in, gain_ffn_out, gain_query, gain_key]
    ).reshape(-1, LANES)
    gain_rel = gains[None]
    for bit in (1, 2):
        gain_rel = jnp.concatenate([gain_rel, permuted(gain_rel, "fsdp", bit)], axis=0)
    gain_all = jnp.stack(
        [lax.dynamic_index_in_dim(gain_rel, at ^ place, 0, keepdims=False) for at in range(blocks)]
    ).reshape(blocks, -1).astype(jnp.float32)
    norm_attn_in = gain_all[:, :shard_d].reshape(-1)
    norm_attn_out = gain_all[:, shard_d : 2 * shard_d].reshape(-1)
    norm_ffn_in = gain_all[:, 2 * shard_d : 3 * shard_d].reshape(-1)
    norm_ffn_out = gain_all[:, 3 * shard_d : 4 * shard_d].reshape(-1)
    key_part = gain_query.shape[0]
    norm_query = gain_all[:, 4 * shard_d : 4 * shard_d + key_part].reshape(-1)
    norm_key = gain_all[:, 4 * shard_d + key_part :].reshape(-1)

    first_flat = to_slabs(jnp.concatenate([w_query, w_key, w_value], axis=1))
    first_rows = first_flat.shape[0] // 8
    first_piece = lax.dynamic_slice_in_dim(first_flat, seq_at * first_rows, first_rows, 0)
    first_stages = gather_stages(first_piece, pair_gather)
    next(first_stages)
    next(first_stages)
    first_rel = next(first_stages)
    seq_order = [(at % 2) * 4 + at // 2 for at in range(8)]
    first_all = jnp.stack(
        [lax.dynamic_index_in_dim(first_rel, at ^ own_place, 0, keepdims=False) for at in seq_order],
        axis=1,
    )
    first_width = w_query.shape[1] + w_key.shape[1] + w_value.shape[1]
    qkv_mat = (
        first_all.reshape(blocks, first_width // LANES, shard_d, LANES)
        .transpose(0, 2, 1, 3)
        .reshape(model, first_width)
    )
    q_wide, k_wide = w_query.shape[1], w_key.shape[1]
    query_mat = qkv_mat[:, :q_wide]
    key_mat = qkv_mat[:, q_wide : q_wide + k_wide]
    value_mat = qkv_mat[:, q_wide + k_wide :]

    def ff_part(weight):
        weight = after(weight, first_rel)
        parts = [
            lax.dynamic_slice_in_dim(weight, block * shard_ff + seq_at * unit, unit, 1)
            for block in range(blocks)
        ]
        return jnp.concatenate(
            [jnp.concatenate(parts[at : at + 2], axis=1) for at in range(0, blocks, 2)], axis=0
        )

    gate_piece, up_piece = ff_part(w_gate), ff_part(w_up)
    down_piece = to_slabs(lax.dynamic_slice_in_dim(w_down, seq_at * unit, unit, 0))
    out_part = shard_hd // 8
    out_piece = to_slabs(lax.dynamic_slice_in_dim(w_out, seq_at * out_part, out_part, 0))
    n_gate, n_down, n_out = gate_piece.shape[0], down_piece.shape[0], out_piece.shape[0]
    second_stages = gather_stages(
        jnp.concatenate([gate_piece, up_piece, down_piece, out_piece]), line_gather
    )
    next(second_stages)
    next(second_stages)
    second_rel = next(second_stages)

    slabs_d = model // LANES
    out_rel = second_rel[:, :, 2 * n_gate + n_down :]
    out_mat = (
        jnp.stack(
            [lax.dynamic_index_in_dim(out_rel, at ^ own_place, 0, keepdims=False) for at in seq_order],
            axis=1,
        )
        .reshape(blocks, 8, slabs_d, out_part, LANES)
        .transpose(0, 1, 3, 2, 4)
        .reshape(-1, model)
    )
    inputs = tokens[0].astype(jnp.float32)
    length = inputs.shape[0]
    head_dim = key_mat.shape[1]
    heads = query_mat.shape[1] // head_dim
    offset = lax.axis_index("seq") * length
    cosine, sine_part = rope_angles(offset + jnp.arange(length, dtype=jnp.int32), head_dim)

    def query_shape(raw_rows, gain_vec):
        return rotate(
            rms_scale(raw_rows.reshape(length, heads, head_dim), gain_vec),
            cosine[:, None, :],
            sine_part[:, None, :],
        )

    def key_shape(raw_rows, gain_vec):
        return rotate(rms_scale(raw_rows, gain_vec), cosine, sine_part)

    attn_normed = rms_scale(inputs, norm_attn_in)
    attn_input = attn_normed.astype(jnp.bfloat16)
    query_pre = jnp.dot(attn_input, query_mat, preferred_element_type=jnp.float32)
    key_pre = jnp.dot(attn_input, key_mat, preferred_element_type=jnp.float32)
    value_rows = jnp.dot(attn_input, value_mat, preferred_element_type=jnp.float32).astype(
        jnp.bfloat16
    )
    query_turned = query_shape(query_pre, norm_query)
    key_turned = key_shape(key_pre, norm_key)
    query_rot = query_turned.astype(jnp.bfloat16)
    key_rot = key_turned.astype(jnp.bfloat16)
    tail_rows = jnp.stack([key_rot[length - WINDOW :], value_rows[length - WINDOW :]])
    tail_prev = passed_along(tail_rows, "seq", 1)
    key_all = jnp.concatenate([tail_prev[0], key_rot], axis=0)
    value_all = jnp.concatenate([tail_prev[1], value_rows], axis=0)
    id_row = document_ids[0]
    pad_ids = jnp.concatenate([jnp.full((WINDOW,), -1, jnp.int32), id_row], axis=0)
    key_ids = lax.dynamic_slice_in_dim(pad_ids, offset, length + WINDOW, 0)
    query_ids = lax.dynamic_slice_in_dim(id_row, offset, length, 0)
    offsets = (
        jnp.arange(QBLK + WINDOW, dtype=jnp.int32)[None, :]
        - jnp.arange(QBLK, dtype=jnp.int32)[:, None]
    )
    inside = (offsets >= 1) & (offsets <= WINDOW)
    block_starts = list(range(0, length, QBLK))

    def masked_scores(block_start):
        query_block = query_rot[block_start : block_start + QBLK]
        key_block = key_all[block_start : block_start + QBLK + WINDOW]
        allowed = inside & (
            key_ids[block_start : block_start + QBLK + WINDOW][None, :]
            == query_ids[block_start : block_start + QBLK][:, None]
        )
        scores = (
            jnp.einsum("qhd,kd->hqk", query_block, key_block, preferred_element_type=jnp.float32)
            * score_scale
        )
        return jnp.where(allowed[None], scores, mask_fill)

    head_blocks = []
    for block_start in block_starts:
        masked = masked_scores(block_start)
        row_max = jnp.max(masked, axis=-1, keepdims=True)
        unnormed = jnp.exp(masked - row_max)
        row_total = jnp.sum(unnormed, axis=-1, keepdims=True)
        probs_low = (unnormed / row_total).astype(jnp.bfloat16)
        head_blocks.append(
            jnp.einsum(
                "hqk,kd->qhd",
                probs_low,
                value_all[block_start : block_start + QBLK + WINDOW],
                preferred_element_type=jnp.float32,
            )
        )
    heads_out = (
        jnp.concatenate(head_blocks, axis=0).reshape(length, heads * head_dim).astype(jnp.bfloat16)
    )
    gain_rows = jnp.concatenate(
        [
            jnp.stack([norm_attn_out, norm_ffn_in, norm_ffn_out]),
            jnp.zeros((5, model), jnp.float32),
        ]
    )
    result, middle_grad, heads_low, out_abs, gain_grads, pack_grad = middle_layer(
        heads_out, tokens[0], cotangent[0], gain_rows, out_mat, second_rel, n_gate, n_down, n_out
    )
    gain_ao_grad, gain_fi_grad, gain_fo_grad = gain_grads[0], gain_grads[1], gain_grads[2]
    def seq_to_rel(parts):
        rel = [j ^ own_place for j in range(8)]
        return jnp.stack(
            [
                lax.dynamic_index_in_dim(parts, (p % 4) * 2 + p // 4, 0, keepdims=False)
                for p in rel
            ]
        )

    second_parts = jnp.concatenate([pack_grad, seq_to_rel(out_abs)], axis=2)
    second_sums = reduce_stages(second_parts, line_reduce)
    query_flat = query_rot.reshape(length, heads * head_dim)
    query_grads, carry = [], None
    own_rows = []
    for block_index, _ in enumerate(block_starts):
        if block_index == 1:
            heads_low = after(heads_low, next(second_sums))
        dq, dk, dv = attention_back(
            query_flat, heads_low, key_all, value_all, query_ids, key_ids, block_index
        )
        query_grads.append(dq)
        both = jnp.concatenate([dk, dv], axis=1)
        if carry is None:
            tail_next = passed_along(both[:WINDOW].astype(jnp.bfloat16), "seq", -1)
        else:
            own_rows.append(both[:WINDOW] + carry)
        carry = both[WINDOW:]
    own_rows.append(carry + tail_next.astype(jnp.float32))
    own_all = jnp.concatenate(own_rows, axis=0)
    gain_row = jnp.concatenate([norm_attn_in[None], jnp.zeros((7, model), jnp.float32)])
    gain_heads = jnp.concatenate(
        [norm_query[None], norm_key[None], jnp.zeros((6, head_dim), jnp.float32)]
    )
    gain_row = after(gain_row, *next(second_sums))
    input_grad, first_flat_grad, gain_in_grads, gain_head_grads = projection_back(
        tokens[0],
        middle_grad,
        jnp.concatenate(query_grads, axis=0),
        own_all[:, :head_dim],
        own_all[:, head_dim:],
        cosine,
        sine_part,
        gain_row,
        gain_heads,
        qkv_mat,
        blocks,
        first_rows,
    )
    gain_ai_grad = gain_in_grads[0]
    gain_q_grad, gain_k_grad = gain_head_grads[0], gain_head_grads[1]
    gain_parts = jnp.concatenate(
        [
            jnp.stack([gain_ai_grad, gain_ao_grad, gain_fi_grad, gain_fo_grad])
            .reshape(4, blocks, shard_d)
            .transpose(1, 0, 2)
            .reshape(blocks, -1),
            gain_q_grad.reshape(blocks, -1),
            gain_k_grad.reshape(blocks, -1),
        ],
        axis=1,
    )
    gain_width = gain_parts.shape[1] // 8
    gain_parts = gain_parts.reshape(blocks, 8, 1, gain_width).transpose(1, 0, 2, 3)
    gain_parts = jnp.pad(
        gain_parts, ((0, 0), (0, 0), (0, 15), (0, LANES - gain_width))
    ).astype(jnp.bfloat16)
    first_parts = seq_to_rel(jnp.concatenate([first_flat_grad, gain_parts], axis=2))
    first_parts = after(first_parts, next(second_sums))
    first_sums = reduce_stages(first_parts, pair_reduce)
    for _ in range(3):
        next(first_sums)
    first_final = next(first_sums)
    second_final = next(second_sums)
    order = jnp.stack([at ^ own_place for at in seq_order]).astype(jnp.int32)
    query_own, key_own_w, value_own_w = unpacked(
        lambda *refs: first_kernel(*refs, rows=first_rows),
        order,
        first_final,
        [w_query.shape, w_key.shape, w_value.shape],
        "first_own",
    )
    out_own, gate_own, up_own, down_own = unpacked(
        second_kernel,
        order,
        second_final,
        [w_out.shape, w_gate.shape, w_up.shape, w_down.shape],
        "second_own",
    )
    gain_final = jnp.stack(
        [
            lax.dynamic_slice(first_final, (order[at], first_rows, 0), (1, 1, LANES))[0, 0]
            for at in range(8)
        ]
    )
    gain_own = gain_final[:, :gain_width].reshape(-1).astype(jnp.float32)
    finals = (
        query_own,
        key_own_w,
        value_own_w,
        out_own,
        gate_own,
        up_own,
        down_own,
        gain_own[:shard_d],
        gain_own[shard_d : 2 * shard_d],
        gain_own[2 * shard_d : 3 * shard_d],
        gain_own[3 * shard_d : 4 * shard_d],
        gain_own[4 * shard_d : 4 * shard_d + key_part],
        gain_own[4 * shard_d + key_part :],
    )
    return (
        result[None],
        input_grad[None],
        finals[0],
        finals[1],
        finals[2],
        finals[3],
        finals[4],
        finals[5],
        finals[6],
        finals[7],
        finals[8],
        finals[9],
        finals[10],
        finals[11],
        finals[12],
    )


def solution(mesh):
    fits = mesh.shape["seq"] == 8 and mesh.shape["fsdp"] == 4
    placed = (
        P("fsdp", "seq", None),
        P("fsdp", None),
        P("fsdp", "seq", None),
        P("fsdp", None),
        P("fsdp", None),
        P("fsdp", None),
        P("fsdp", None),
        P("fsdp", None),
        P("fsdp", None),
        P("fsdp", None),
        P("fsdp"),
        P("fsdp"),
        P("fsdp"),
        P("fsdp"),
        P("fsdp"),
        P("fsdp"),
    )
    return jax.shard_map(
        local_fast if fits else local_generic,
        mesh=mesh,
        in_specs=placed,
        out_specs=(
            P("fsdp", "seq", None),
            P("fsdp", "seq", None),
            P("fsdp", None),
            P("fsdp", None),
            P("fsdp", None),
            P("fsdp", None),
            P("fsdp", None),
            P("fsdp", None),
            P("fsdp", None),
            P("fsdp"),
            P("fsdp"),
            P("fsdp"),
            P("fsdp"),
            P("fsdp"),
            P("fsdp"),
        ),
        check_vma=False,
    )
```
